128 devices in a mesh: gx: 16 (over z, y), gy: 8 (over x, core).
Axes of the slice: x: 4, y: 4, z: 4, core: 2. Of those that a mesh axis runs over, the one named last changes fastest.
Arguments:
- thermal_grid: float32 [64, 128, 128], P('gx', 'gy'), may hold values from -6 to 6
- average_blend_fraction: float32 [64, 128, 128], P('gx', 'gy'), may hold values from 0.05 to 0.95
- normalized_blend_variance: float32 [64, 128, 128], P('gx', 'gy'), may hold values from 0.002 to 0.5
- small_volume_mass: float32 [64, 128, 128], P('gx', 'gy'), may hold values from 0.01 to 0.1
- bare_scalar_decay: float32 [64, 128, 128], P('gx', 'gy'), may hold values from 0.05 to 1
- parent_block: int32 [64, 128, 128], P('gx', 'gy'), may hold values from 0 to 511, as said below
- species_given_block: float32 [512, 16, 128], P(('gx', 'gy')), may hold values from -6 to 6
- block_position: int32 [512], replicated, may hold values from 0 to 511, each once
- face_partners: int32 [512, 6], replicated, may hold values from 0 to 511, as said below
- reaction_increments: int32 [512], replicated, may hold values from 0 to 15, as said below
- chemical_coupling: float32 [16, 16], replicated, may hold values from -1.5 to 1.5
- species_thermal_weight: float32 [16], replicated, may hold values from -1.5 to 1.5
Outputs:
- species_next: float32 [512, 16, 128], P(('gx', 'gy'))
- temperature_next: float32 [64, 128, 128], P('gx', 'gy')
The draws below stay inside these ranges and needn't reach their ends.
Inputs may be any that keep to these rules, and one draw needn't show every extreme that they name: `parent_block`: each fine cell names the coarse cell under it after a shift of at most 2 fine cells along each dimension; every coarse cell is named. `face_partners`: A cell on the grid's border names itself in place of a missing neighbour; every coarse cell is named. `reaction_increments`: both ends are reached in every draw.
All inputs are finite; a program needn't handle non-finite values.
Results may differ from the reference program's by a relative error of at most 0.0003.
Values sent between devices are 32-bit elements; how exact they have to be, the bound alone decides.
No kernel may reach another device: no remote copies, remote signals or barrier semaphores. Data moves between devices by JAX's collectives and lax.ppermute only.
A program may use at most 128 MiB of HBM per device.

```python
import math
import jax
import jax.numpy as jnp
from jax import lax

SMALL_ALONG_Z = 128
ETA = 128
SPEC = 16
SUBMAX = 16
STEPS = 2
JITTER = 2
CGZ = 8
CGX = 8
CGY = 8
BLOCK_COUNT = 512
SMALL_ALONG_X = 64
SMALL_ALONG_Y = 128


def numbering(key):
    return jax.random.permutation(jax.random.fold_in(key, 5), BLOCK_COUNT).astype(jnp.int32)


def parents(key):
    perm = numbering(key)
    shifts = jax.random.randint(jax.random.fold_in(key, 11), (3, SMALL_ALONG_X, SMALL_ALONG_Y, SMALL_ALONG_Z), -JITTER, JITTER + 1)
    xs = jnp.clip(jnp.arange(SMALL_ALONG_X)[:, None, None] + shifts[0], 0, SMALL_ALONG_X - 1)
    ys = jnp.clip(jnp.arange(SMALL_ALONG_Y)[None, :, None] + shifts[1], 0, SMALL_ALONG_Y - 1)
    zs = jnp.clip(jnp.arange(SMALL_ALONG_Z)[None, None, :] + shifts[2], 0, SMALL_ALONG_Z - 1)
    coarse = (xs // (SMALL_ALONG_X // CGX) * CGY + ys // (SMALL_ALONG_Y // CGY)) * CGZ + zs // (SMALL_ALONG_Z // CGZ)
    return perm[coarse].astype(jnp.int32)


def narrow_cells(key):
    owner = parents(key)
    picked = jax.random.permutation(jax.random.fold_in(key, 21), BLOCK_COUNT) < BLOCK_COUNT // 4
    sides = jax.random.randint(jax.random.fold_in(key, 22), (BLOCK_COUNT,), 0, 2)
    return (picked[owner], sides[owner])


def fresh_uniform(key, salt):
    return jax.random.uniform(jax.random.fold_in(key, salt), (SMALL_ALONG_X, SMALL_ALONG_Y, SMALL_ALONG_Z), jnp.float32)


def draw_parent_block(key, part):
    return parents(key)


def draw_average_blend_fraction(key, part):
    picked, sides = narrow_cells(key)
    base = fresh_uniform(key, 31)
    spread = 0.05 + 0.9 * base
    ends = 0.05 + 0.9 * sides.astype(jnp.float32)
    return jnp.clip(jnp.where(picked, ends, spread), 0.05, 0.95).astype(jnp.float32)


def draw_normalized_blend_variance(key, part):
    picked, sides = narrow_cells(key)
    base = fresh_uniform(key, 32)
    spread = jnp.exp(jnp.log(0.002) + base * (jnp.log(0.5) - jnp.log(0.002)))
    return jnp.clip(jnp.where(picked, 0.002, spread), 0.002, 0.5).astype(jnp.float32)


def draw_bare_scalar_decay(key, part):
    picked, sides = narrow_cells(key)
    base = fresh_uniform(key, 33)
    spread = jnp.exp(jnp.log(0.05) + base * (0.0 - jnp.log(0.05)))
    return jnp.clip(jnp.where(picked, 1.0, spread), 0.05, 1.0).astype(jnp.float32)


def draw_face_partners(key, part):
    perm = numbering(key)
    geo = jnp.arange(BLOCK_COUNT)
    cxs = geo // (CGY * CGZ)
    cys = geo // CGZ % CGY
    czs = geo % CGZ
    columns = []
    for axis_pick, offset in ((0, 1), (0, -1), (1, 1), (1, -1), (2, 1), (2, -1)):
        nx_cell = jnp.clip(cxs + offset, 0, CGX - 1) if axis_pick == 0 else cxs
        ny_cell = jnp.clip(cys + offset, 0, CGY - 1) if axis_pick == 1 else cys
        nz_cell = jnp.clip(czs + offset, 0, CGZ - 1) if axis_pick == 2 else czs
        columns.append((nx_cell * CGY + ny_cell) * CGZ + nz_cell)
    near_geo = jnp.stack(columns, axis=1)
    result = jnp.zeros((BLOCK_COUNT, 6), jnp.int32).at[perm].set(perm[near_geo])
    return result.astype(jnp.int32)


def draw_reaction_increments(key, part):
    first = jax.random.randint(jax.random.fold_in(key, 3), (BLOCK_COUNT,), 0, SUBMAX)
    second = jax.random.randint(jax.random.fold_in(key, 4), (BLOCK_COUNT,), 0, SUBMAX)
    values = first * second // (SUBMAX - 1)
    spots = jax.random.randint(jax.random.fold_in(key, 6), (2,), 0, BLOCK_COUNT // 2)
    values = values.at[spots[0]].set(SUBMAX - 1)
    values = values.at[BLOCK_COUNT // 2 + spots[1]].set(0)
    return values.astype(jnp.int32)


def block_levels(own_key, extent, cuts, low, largest):
    gain = 1.0
    for axis_at, blocks in cuts:
        steps = jax.random.uniform(jax.random.fold_in(jax.random.fold_in(own_key, 6), axis_at), (blocks,), jnp.float32, low / len(cuts), largest / len(cuts))
        gain = gain * jnp.repeat(jnp.exp(steps), extent[axis_at] // blocks).reshape((-1,) + (1,) * (len(extent) - 1 - axis_at))
    return gain


def normal_values(rng, extent, scale, reach, pieces=(), kind=jnp.bfloat16):
    values = jax.random.normal(rng, extent, jnp.float32) * scale
    if len(pieces) > 0:
        values = block_levels(rng, extent, pieces, -0.22, 0.18) * values
    return jnp.clip(values, min=-reach, max=reach).astype(kind)


def setup_inputs(seed: int = 0) -> dict:
    seeds = jax.random.split(jax.random.key(seed), 13)
    thermal_grid = normal_values(seeds[0], (SMALL_ALONG_X, SMALL_ALONG_Y, SMALL_ALONG_Z), 1.0, 6.0, ((0, 16), (1, 8)), jnp.float32)
    average_blend_fraction = draw_average_blend_fraction(jax.random.fold_in(seeds[12], 71), 0)
    normalized_blend_variance = draw_normalized_blend_variance(jax.random.fold_in(seeds[12], 71), 0)
    small_volume_mass = jnp.clip(jnp.exp(math.log(0.1) - 2.3025851 * jax.random.uniform(seeds[3], (SMALL_ALONG_X, SMALL_ALONG_Y, SMALL_ALONG_Z), jnp.float32) ** block_levels(seeds[3], (SMALL_ALONG_X, SMALL_ALONG_Y, SMALL_ALONG_Z), ((0, 16), (1, 8)), -0.2, 0.2)), 0.01, 0.1)
    bare_scalar_decay = draw_bare_scalar_decay(jax.random.fold_in(seeds[12], 71), 0)
    parent_block = draw_parent_block(jax.random.fold_in(seeds[12], 71), 0)
    species_given_block = normal_values(seeds[6], (BLOCK_COUNT, SPEC, ETA), 1.0, 6.0, ((0, 128),), jnp.float32)
    block_position = jax.random.permutation(seeds[7], BLOCK_COUNT).astype(jnp.int32)
    face_partners = draw_face_partners(jax.random.fold_in(seeds[12], 71), 0)
    reaction_increments = draw_reaction_increments(jax.random.fold_in(seeds[12], 71), 0)
    chemical_coupling = normal_values(seeds[10], (SPEC, SPEC), SPEC ** -0.5, 1.5, (), jnp.float32)
    species_thermal_weight = normal_values(seeds[11], (SPEC,), SPEC ** -0.5, 1.5, (), jnp.float32)
    return {"thermal_grid": thermal_grid, "average_blend_fraction": average_blend_fraction, "normalized_blend_variance": normalized_blend_variance, "small_volume_mass": small_volume_mass, "bare_scalar_decay": bare_scalar_decay, "parent_block": parent_block, "species_given_block": species_given_block, "block_position": block_position, "face_partners": face_partners, "reaction_increments": reaction_increments, "chemical_coupling": chemical_coupling, "species_thermal_weight": species_thermal_weight}


coupling = 0.05
mixing_rate = 0.2
react_rate = 0.5
prior_weight = 1.0
prior_flux = 0.5
thermal_diffusion = 0.1
damping_contribution = 0.3


def beta_table(average_blend_fraction, normalized_blend_variance):
    points = (jnp.arange(ETA, dtype=jnp.float32) + 0.5) / ETA
    shape_sum = 1.0 / normalized_blend_variance - 1.0
    alpha = average_blend_fraction * shape_sum
    beta_b = (1.0 - average_blend_fraction) * shape_sum
    logits = (alpha - 1.0)[..., None] * jnp.log(points) + (beta_b - 1.0)[..., None] * jnp.log(1.0 - points)
    return jax.nn.softmax(logits, axis=-1)


def lap_mixture(field):
    bordered_grid = jnp.concatenate([field[..., :1], field, field[..., -1:]], axis=-1)
    return bordered_grid[..., 2:] - 2.0 * field + bordered_grid[..., :-2]


def coarse_advance(fluid_condition, nearby, scalar_decay_speed, counts, chemical_coupling, turns):
    fluid_condition = fluid_condition + coupling * jnp.sum(nearby - fluid_condition[:, None], axis=1)
    fraction = 1.0 / counts.astype(jnp.float32)

    def substep(index, current):
        source = jnp.einsum("st,ctk->csk", chemical_coupling, jnp.tanh(current), precision=lax.Precision.HIGHEST)
        update = fraction[:, None, None] * (mixing_rate * scalar_decay_speed[:, None, :] * lap_mixture(current) + react_rate * source)
        return jnp.where((index < counts)[:, None, None], current + update, current)

    return lax.fori_loop(0, turns, substep, fluid_condition)


def small_volume_accumulations(average_blend_fraction, normalized_blend_variance, small_volume_mass, bare_scalar_decay, thermal_grid, parent_block, block_numbers):
    def attach_line(overall_aggregate, row):
        zm_row, zs_row, wt_row, cb_row, tp_row, ids_row = row
        tabulated_values = beta_table(zm_row, zs_row).reshape(-1, ETA)
        weighted = wt_row.reshape(-1, 1) * tabulated_values
        scalar_decay_speed = (cb_row * (1.0 + 0.5 * jnp.tanh(tp_row))).reshape(-1, 1)
        values = jnp.stack([weighted, weighted * scalar_decay_speed], axis=1)
        return overall_aggregate + jax.ops.segment_sum(values, ids_row.reshape(-1), num_segments=block_numbers), None

    first_shift_amount = jnp.zeros((block_numbers, 2, ETA), jnp.float32)
    overall_aggregate, discarded_quantity = lax.scan(attach_line, first_shift_amount, (average_blend_fraction, normalized_blend_variance, small_volume_mass, bare_scalar_decay, thermal_grid, parent_block))
    return overall_aggregate


def reverse_quadrature(average_blend_fraction, normalized_blend_variance, parent_block, blend_block_number):
    def one_row(row):
        zm_row, zs_row, ids_row = row
        tabulated_values = beta_table(zm_row, zs_row)
        return jnp.sum(tabulated_values * blend_block_number[ids_row], axis=-1)

    return lax.map(one_row, (average_blend_fraction, normalized_blend_variance, parent_block))


def small_grid_renewal(thermal_grid, small_grid_thermal):
    bordered_grid = jnp.pad(thermal_grid, 1)
    nearby_blocks = bordered_grid[2:, 1:-1, 1:-1] + bordered_grid[:-2, 1:-1, 1:-1]
    nearby_blocks = nearby_blocks + bordered_grid[1:-1, 2:, 1:-1] + bordered_grid[1:-1, :-2, 1:-1]
    nearby_blocks = nearby_blocks + bordered_grid[1:-1, 1:-1, 2:] + bordered_grid[1:-1, 1:-1, :-2]
    return thermal_grid + thermal_diffusion * (nearby_blocks - 6.0 * thermal_grid) + damping_contribution * (small_grid_thermal - thermal_grid)


def reference(thermal_grid, average_blend_fraction, normalized_blend_variance, small_volume_mass, bare_scalar_decay, parent_block, species_given_block, block_position, face_partners, reaction_increments, chemical_coupling, species_thermal_weight):
    position_block_map = jnp.argsort(block_position).astype(jnp.int32)
    near_slot = block_position[face_partners[position_block_map]]
    counts = reaction_increments[position_block_map] + 1
    fluid_condition = species_given_block
    for turn in range(STEPS):
        local_aggregates = small_volume_accumulations(average_blend_fraction, normalized_blend_variance, small_volume_mass, bare_scalar_decay, thermal_grid, parent_block, BLOCK_COUNT)[position_block_map]
        cchi = (local_aggregates[:, 1] + prior_flux) / (local_aggregates[:, 0] + prior_weight)
        fluid_condition = coarse_advance(fluid_condition, fluid_condition[near_slot], cchi, counts, chemical_coupling, SUBMAX)
        reduced_thermal = jnp.einsum("s,csk->ck", species_thermal_weight, fluid_condition, precision=lax.Precision.HIGHEST)
        small_grid_thermal = reverse_quadrature(average_blend_fraction, normalized_blend_variance, parent_block, reduced_thermal[block_position])
        thermal_grid = small_grid_renewal(thermal_grid, small_grid_thermal)
    return fluid_condition, thermal_grid
```

```python
import jax
import jax.numpy as jnp
from jax import lax
from jax.experimental import pallas as pl
from jax.experimental.pallas import tpu as pltpu
from jax.sharding import PartitionSpec as P

DEV = 128
OWN = 4
SLOTS = 512
SPEC = 16
ETA = 128
ROWS = 64
SUBMAX = 16
LABELS = 48
GROUPS = 8
WIDE = 1024
FIRST = 9
LATER = 5

coupling = 0.05
mixing_rate = 0.2
react_rate = 0.5
prior_weight = 1.0
prior_flux = 0.5
thermal_diffusion = 0.1
damping_contribution = 0.3

f32 = jnp.float32
bf16 = jnp.bfloat16
NN = ((1,), (0,))
NT = ((1,), (1,))
TN = ((0,), (0,))


def dot(a, b, dims):
    return lax.dot_general(a, b, (dims, ((), ())), preferred_element_type=f32)


def iota(shape, dim):
    return lax.broadcasted_iota(jnp.int32, shape, dim)


def halves(x):
    high = x.astype(bf16)
    return high, (x - high.astype(f32)).astype(bf16)


def thirds(x):
    high = x.astype(bf16)
    rest = x - high.astype(f32)
    mid = rest.astype(bf16)
    return high, mid, (rest - mid.astype(f32)).astype(bf16)


def hot(mask):
    return jnp.where(mask, 1.0, 0.0).astype(bf16)


def rows_of(ref, group):
    return ref[pl.ds(pl.multiple_of(group * 8, 8), 8), :]


def put_rows(ref, group, rows):
    ref[pl.ds(pl.multiple_of(group * 8, 8), 8), :] = jnp.concatenate(rows, axis=0)


def to_slots(rs, sums):
    high, mid, low = thirds(sums)
    return dot(rs, high, NN) + dot(rs, mid, NN) + dot(rs, low, NN)


def prep_kernel(
    t_ref, av_ref, var_ref, mass_ref, bare_ref, par_ref, bp_ref, fp_ref,
    e_ref, mw_ref, rinv_ref, lab_ref, rs_ref, m_ref, sums_ref,
    pres, le, l1e, a1, b1, chi, arms, acc,
):
    for block in range(4):
        ids = iota((128, 128), 0) + block * 128

        def seen(group, found):
            rows = rows_of(par_ref, group)
            for q in range(8):
                found = jnp.where(rows[q : q + 1] == ids, 1.0, found)
            return found

        found = lax.fori_loop(0, GROUPS, seen, jnp.zeros((128, 128), f32))
        pres[block * 128 : (block + 1) * 128, :] = found.astype(bf16)
    named = dot(pres[...], jnp.ones((128, 128), bf16), NN) > 0.5
    before = hot(iota((SLOTS, SLOTS), 1) < iota((SLOTS, SLOTS), 0))
    rank = dot(before, hot(named), NN)
    sel = hot(named & (rank == iota((SLOTS, 128), 1).astype(f32)))
    cell = iota((SLOTS, 128), 0) + 1
    upper = dot(sel, (cell >> 4).astype(f32).astype(bf16), TN)
    lower = dot(sel, (cell & 15).astype(f32).astype(bf16), TN)
    label = (upper * 16.0 + lower).astype(jnp.int32) - 1
    lab = label[:LABELS]
    lab_ref[...] = lab

    place = iota((SLOTS, SLOTS), 0)
    place = (place & 127) * OWN + (place >> 7)
    pt = hot(bp_ref[...] == place)
    rs = dot(pt, sel, NN).astype(bf16)[:, :LABELS]
    rs_ref[...] = rs
    other = iota((SLOTS, SLOTS), 1)
    adjacent = jnp.zeros((SLOTS, SLOTS), f32)
    for j in range(6):
        adjacent = adjacent + jnp.where(fp_ref[:, j : j + 1] == other, 1.0, 0.0)
    half = dot(pt, adjacent.astype(bf16), NN).astype(bf16)
    m_ref[...] = dot(half, pt, NT).astype(bf16)

    point = (iota((ETA, 128), 0).astype(f32) + 0.5) / ETA
    le[...] = jnp.log(point)
    l1e[...] = jnp.log(1.0 - point)
    shape_sum = 1.0 / var_ref[...] - 1.0
    a1[...] = av_ref[...] * shape_sum - 1.0
    b1[...] = (1.0 - av_ref[...]) * shape_sum - 1.0
    chi[...] = bare_ref[...] * (1.0 + 0.5 * jnp.tanh(t_ref[...]))
    acc[...] = jnp.zeros_like(acc)

    def tables(group, carry):
        a_rows, b_rows = rows_of(a1, group), rows_of(b1, group)
        chi_rows, mass_rows, par_rows = rows_of(chi, group), rows_of(mass_ref, group), rows_of(par_ref, group)
        inverse, mass_over = [], []
        for q in range(8):
            at = slice(q * 128, (q + 1) * 128)
            logits = a_rows[q : q + 1] * le[...] + b_rows[q : q + 1] * l1e[...]
            table = jnp.exp(logits - jnp.max(logits, axis=0, keepdims=True))
            r = 1.0 / jnp.sum(table, axis=0, keepdims=True)
            high, low = halves(table)
            e_ref[group, 0:128, at] = high
            e_ref[group, 128:256, at] = low
            w = mass_rows[q : q + 1] * r
            n = w * chi_rows[q : q + 1]
            inverse.append(r)
            mass_over.append(w)
            mine = lab == par_rows[q : q + 1]
            for k, part in enumerate((*halves(w), *halves(n))):
                arms[k * LABELS : (k + 1) * LABELS, at] = jnp.where(mine, part.astype(f32), 0.0).astype(bf16)
        put_rows(rinv_ref, group, inverse)
        put_rows(mw_ref, group, mass_over)
        acc[...] += dot(arms[...], e_ref[group], NT)
        return carry

    lax.fori_loop(0, GROUPS, tables, 0)
    both = acc[:, :128] + acc[:, 128:]
    w48 = both[0:48] + both[48:96]
    n48 = both[96:144] + both[144:192]
    sums_ref[...] = to_slots(rs, jnp.concatenate([w48, n48], axis=1))


def neighbour_sums(part, m):
    lane = iota((128, 128), 1)
    stacked = jnp.concatenate([jnp.where(lane >> 4 == t, part, 0.0) for t in range(OWN)], axis=0)
    high, low = halves(stacked)
    both = dot(m, jnp.concatenate([high, low], axis=1), NN)
    total = both[:, :128] + both[:, 128:]
    for shift in (64, 32, 16):
        total = total + pltpu.roll(total, shift, 1)
    out = jnp.zeros((128, 128), f32)
    for t in range(OWN):
        out = jnp.where(lane >> 4 == t, total[t * 128 : (t + 1) * 128], out)
    return out


def edges_by_z(t_ref, edge):
    edge[...] = jnp.zeros_like(edge)
    edge[64:80, :] = t_ref[0:16, :]
    edge[80:96, :] = t_ref[48:64, :]
    for x in range(4):
        edge[96 + x : 97 + x, :] = t_ref[16 * x : 16 * x + 1, :]
        edge[100 + x : 101 + x, :] = t_ref[16 * x + 15 : 16 * x + 16, :]
    return edge[...].T


def first_pack_kernel(got_ref, m_ref, sums_ref, t_ref, out_ref, edge):
    misc = neighbour_sums(got_ref[...], m_ref[...]) + edges_by_z(t_ref, edge)
    for t in range(OWN):
        out_ref[pl.ds(t, 128, stride=FIRST), :] = sums_ref[t * 128 : (t + 1) * 128, 0:128]
        out_ref[pl.ds(OWN + t, 128, stride=FIRST), :] = sums_ref[t * 128 : (t + 1) * 128, 128:256]
    out_ref[pl.ds(2 * OWN, 128, stride=FIRST), :] = misc


def passed_on(misc):
    lane, row = iota((128, 128), 1), iota((128, 128), 0)
    gx, gy = row >> 3, row & 7
    out = jnp.where((lane >= 64) & (lane < 80) & (gx < 15), pltpu.roll(misc, 120, 0), 0.0)
    out = jnp.where((lane >= 80) & (lane < 96) & (gx > 0), pltpu.roll(misc, 8, 0), out)
    out = jnp.where((lane >= 96) & (lane < 100) & (gy < 7), pltpu.roll(misc, 127, 0), out)
    return jnp.where((lane >= 100) & (lane < 104) & (gy > 0), pltpu.roll(misc, 1, 0), out)


def advance(state_ref, misc, cchi, dev, bp_ref, ri_ref, c_ref, sw_ref, cols, out_ref, last):
    for s in range(SPEC):
        cols[s] = jnp.broadcast_to(c_ref[:, s : s + 1], (SPEC, ETA))
    mine = bp_ref[...] == dev * OWN + (iota((ROWS, SLOTS), 0) >> 4)
    count = jnp.sum(jnp.where(mine, ri_ref[...] + 1, 0).astype(f32), axis=1, keepdims=True)
    count = jnp.broadcast_to(count, (ROWS, ETA))
    fraction = 1.0 / count
    mixing = fraction * mixing_rate * jnp.concatenate(
        [jnp.broadcast_to(cchi[t], (SPEC, ETA)) for t in range(OWN)], axis=0
    )
    reacting = fraction * react_rate
    near = misc.T[:ROWS]
    state = state_ref[...]
    state = state + coupling * (near - 6.0 * state)
    lane = iota((ROWS, ETA), 1)

    def substep(index, current):
        speed = jnp.tanh(current)
        source = []
        for t in range(OWN):
            parts = [speed[t * SPEC + s : t * SPEC + s + 1] * cols[s] for s in range(SPEC)]
            while len(parts) > 1:
                parts = [a + b for a, b in zip(parts[::2], parts[1::2])]
            source.append(parts[0])
        source = jnp.concatenate(source, axis=0)
        left = jnp.where(lane == 0, current, pltpu.roll(current, 1, 1))
        right = jnp.where(lane == ETA - 1, current, pltpu.roll(current, ETA - 1, 1))
        update = mixing * (right - 2.0 * current + left) + reacting * source
        return jnp.where(index.astype(f32) < count, current + update, current)

    state = lax.fori_loop(0, SUBMAX, substep, state)
    state_ref_out, pay = out_ref
    state_ref_out[...] = state
    weight = jnp.sum(
        jnp.where(iota((SPEC, SPEC), 0) == iota((SPEC, SPEC), 1), sw_ref[...], 0.0), axis=1, keepdims=True
    )
    for t in range(OWN):
        theta = jnp.sum(weight * state[t * SPEC : (t + 1) * SPEC], axis=0, keepdims=True)
        pay[pl.ds(t, 128, stride=LATER), :] = jnp.broadcast_to(theta, (128, ETA))
    out = passed_on(misc)
    if not last:
        out = out + jnp.concatenate([state, jnp.zeros((128 - ROWS, ETA), f32)], axis=0).T
    pay[pl.ds(OWN, 128, stride=LATER), :] = out


def total_of(got_ref, row, stride):
    return jnp.sum(got_ref[pl.ds(row, 128, stride=stride), :], axis=0, keepdims=True)


def first_advance_kernel(
    dev_ref, got_ref, state_ref, bp_ref, ri_ref, c_ref, sw_ref, state_out, weight_out, pay, cols
):
    cchi = []
    for t in range(OWN):
        w = total_of(got_ref, t, FIRST)
        n = total_of(got_ref, OWN + t, FIRST)
        weight_out[t : t + 1, :] = w
        cchi.append((n + prior_flux) / (w + prior_weight))
    misc = got_ref[pl.ds(2 * OWN, 128, stride=FIRST), :]
    advance(state_ref, misc, cchi, dev_ref[0], bp_ref, ri_ref, c_ref, sw_ref, cols, (state_out, pay), False)


def later_advance_kernel(
    dev_ref, got_ref, state_ref, weight_ref, bp_ref, ri_ref, c_ref, sw_ref, state_out, pay, cols
):
    cchi = []
    for t in range(OWN):
        n = total_of(got_ref, t, LATER)
        cchi.append((n + prior_flux) / (weight_ref[t : t + 1, :] + prior_weight))
    misc = got_ref[pl.ds(OWN, 128, stride=LATER), :]
    advance(state_ref, misc, cchi, dev_ref[0], bp_ref, ri_ref, c_ref, sw_ref, cols, (state_out, pay), True)


def fine_update(got_ref, misc, t_ref, e_ref, rinv_ref, lab_ref, rs_ref, par_ref, tfine, grid):
    theta = jnp.concatenate([got_ref[pl.ds(t, 128, stride=LATER), :] for t in range(OWN)], axis=0)
    picked = dot(rs_ref[...], jnp.concatenate(halves(theta), axis=1), TN).astype(bf16)
    high, low = picked[:, :128], picked[:, 128:]
    rows = jnp.concatenate(
        [jnp.concatenate([high, high], axis=1), jnp.concatenate([low, low], axis=1)], axis=0
    )
    lab = lab_ref[...]

    def weigh(group, carry):
        means = dot(rows, e_ref[group], NN)
        means = means[:LABELS] + means[LABELS:]
        par_rows, inverse = rows_of(par_ref, group), rows_of(rinv_ref, group)
        out = []
        for q in range(8):
            mine = lab == par_rows[q : q + 1]
            out.append(jnp.sum(jnp.where(mine, means[:, q * 128 : (q + 1) * 128], 0.0), axis=0, keepdims=True))
        put_rows(tfine, group, [jnp.concatenate(out, axis=0) * inverse])
        return carry

    lax.fori_loop(0, GROUPS, weigh, 0)
    beside = misc.T
    t = t_ref[...]
    grid[1:5, 8:24, :] = t.reshape(4, 16, 128)
    grid[5, 8:24, :] = beside[64:80]
    grid[0, 8:24, :] = beside[80:96]
    for x in range(4):
        grid[1 + x, 24:25, :] = beside[96 + x : 97 + x]
        grid[1 + x, 7:8, :] = beside[100 + x : 101 + x]
    around = grid[2:6, 8:24, :] + grid[0:4, 8:24, :]
    around = around + grid[1:5, 9:25, :] + grid[1:5, 7:23, :]
    around = around.reshape(ROWS, 128)
    lane = iota((ROWS, 128), 1)
    around = around + jnp.where(lane == 127, 0.0, pltpu.roll(t, 127, 1))
    around = around + jnp.where(lane == 0, 0.0, pltpu.roll(t, 1, 1))
    return t + thermal_diffusion * (around - 6.0 * t) + damping_contribution * (tfine[...] - t)


def middle_kernel(
    got_ref, t_ref, e_ref, rinv_ref, mw_ref, lab_ref, rs_ref, m_ref, par_ref, bare_ref,
    t_out, pay, tfine, grid, flux, arms, acc, edge,
):
    misc = got_ref[pl.ds(OWN, 128, stride=LATER), :]
    t = fine_update(got_ref, misc, t_ref, e_ref, rinv_ref, lab_ref, rs_ref, par_ref, tfine, grid)
    t_out[...] = t
    flux[...] = mw_ref[...] * (bare_ref[...] * (1.0 + 0.5 * jnp.tanh(t)))
    acc[...] = jnp.zeros_like(acc)
    lab = lab_ref[...]

    def gather(group, carry):
        flux_rows, par_rows = rows_of(flux, group), rows_of(par_ref, group)
        for q in range(8):
            mine = lab == par_rows[q : q + 1]
            for k, part in enumerate(halves(flux_rows[q : q + 1])):
                arms[k * LABELS : (k + 1) * LABELS, q * 128 : (q + 1) * 128] = jnp.where(
                    mine, part.astype(f32), 0.0
                ).astype(bf16)
        acc[...] += dot(arms[...], e_ref[group], NT)
        return carry

    lax.fori_loop(0, GROUPS, gather, 0)
    both = acc[:, :128] + acc[:, 128:]
    sums = to_slots(rs_ref[...], both[0:48] + both[48:96])
    for k in range(OWN):
        pay[pl.ds(k, 128, stride=LATER), :] = sums[k * 128 : (k + 1) * 128]
    out = neighbour_sums(misc, m_ref[...]) + edges_by_z(t_out, edge)
    pay[pl.ds(OWN, 128, stride=LATER), :] = out


def final_kernel(got_ref, t_ref, e_ref, rinv_ref, lab_ref, rs_ref, par_ref, t_out, tfine, grid):
    misc = got_ref[pl.ds(OWN, 128, stride=LATER), :]
    t_out[...] = fine_update(got_ref, misc, t_ref, e_ref, rinv_ref, lab_ref, rs_ref, par_ref, tfine, grid)


def call(kernel, outs, scratch, *operands, scalars=0):
    vmem, smem = pl.BlockSpec(memory_space=pltpu.VMEM), pl.BlockSpec(memory_space=pltpu.SMEM)
    return pl.pallas_call(
        kernel,
        out_shape=[jax.ShapeDtypeStruct(*o) for o in outs],
        in_specs=[smem] * scalars + [vmem] * (len(operands) - scalars),
        out_specs=[vmem] * len(outs),
        scratch_shapes=[pltpu.VMEM(*s) for s in scratch],
    )(*operands)


def exchange(array):
    rows = array.shape[0] // DEV
    sent = array.reshape(DEV, 1, rows * 128)
    return lax.all_to_all(sent, ("gx", "gy"), 0, 0, tiled=True).reshape(array.shape)


def shards(thermal, average, variance, mass, bare, parent, species, position, partners, increments, chem, weight):
    dev = (lax.axis_index("gx") * 8 + lax.axis_index("gy")).astype(jnp.int32).reshape(1)
    fine = [a.reshape(ROWS, 128) for a in (thermal, average, variance, mass, bare, parent)]
    t0, av, var, mass, bare, par = fine
    state = species.reshape(ROWS, ETA)
    bp, ri, sw = position.reshape(1, SLOTS), increments.reshape(1, SLOTS), weight.reshape(1, SPEC)
    cells = ((ROWS, 128), f32)
    square = ((128, 128), f32)
    pay = ((DEV * LATER, 128), f32)

    states = exchange(jnp.pad(state.T, ((0, 0), (0, 128 - ROWS))))
    table, mw, rinv, lab, rs, m, sums = call(
        prep_kernel,
        [((GROUPS, 256, WIDE), bf16), cells, cells, ((LABELS, 128), jnp.int32), ((SLOTS, LABELS), bf16),
         ((SLOTS, SLOTS), bf16), ((SLOTS, 256), f32)],
        [((SLOTS, 128), bf16), square, square, cells, cells, cells, ((4 * LABELS, WIDE), bf16), ((4 * LABELS, 256), f32)],
        t0, av, var, mass, bare, par, bp, partners,
    )
    (sent,) = call(first_pack_kernel, [((DEV * FIRST, 128), f32)], [square], states, m, sums, t0)
    got = exchange(sent)
    cols = ((SPEC, SPEC, ETA), f32)
    state, own_weight, sent = call(
        first_advance_kernel, [((ROWS, ETA), f32), ((8, 128), f32), pay], [cols],
        dev, got, state, bp, ri, chem, sw, scalars=1,
    )
    got = exchange(sent)
    grid = ((6, 32, 128), f32)
    t1, sent = call(
        middle_kernel, [cells, pay],
        [cells, grid, cells, ((2 * LABELS, WIDE), bf16), ((2 * LABELS, 256), f32), square],
        got, t0, table, rinv, mw, lab, rs, m, par, bare,
    )
    got = exchange(sent)
    state, sent = call(
        later_advance_kernel, [((ROWS, ETA), f32), pay], [cols],
        dev, got, state, own_weight, bp, ri, chem, sw, scalars=1,
    )
    got = exchange(sent)
    (t2,) = call(final_kernel, [cells], [cells, grid], got, t1, table, rinv, lab, rs, par)
    return state.reshape(species.shape), t2.reshape(thermal.shape)


def solution(mesh):
    fine = P("gx", "gy", None)
    slots = P(("gx", "gy"), None, None)
    return jax.shard_map(
        shards,
        mesh=mesh,
        in_specs=(fine,) * 6 + (slots,) + (P(),) * 5,
        out_specs=(slots, fine),
        check_vma=False,
    )
```

```python
import jax
import jax.numpy as jnp
from jax import lax
from jax.experimental import pallas as pl
from jax.experimental.pallas import tpu as pltpu
from jax.sharding import PartitionSpec as P

DEV = 128
OWN = 4
SLOTS = 512
SPEC = 16
ETA = 128
ROWS = 64
SUBMAX = 16
LABELS = 48
GROUPS = 8
WIDE = 1024
FIRST = 9
LATER = 5

coupling = 0.05
mixing_rate = 0.2
react_rate = 0.5
prior_weight = 1.0
prior_flux = 0.5
thermal_diffusion = 0.1
damping_contribution = 0.3

f32 = jnp.float32
bf16 = jnp.bfloat16
NN = ((1,), (0,))
NT = ((1,), (1,))
TN = ((0,), (0,))


def dot(a, b, dims):
    return lax.dot_general(a, b, (dims, ((), ())), preferred_element_type=f32)


def iota(shape, dim):
    return lax.broadcasted_iota(jnp.int32, shape, dim)


def halves(x):
    high = x.astype(bf16)
    return high, (x - high.astype(f32)).astype(bf16)


def thirds(x):
    high = x.astype(bf16)
    rest = x - high.astype(f32)
    mid = rest.astype(bf16)
    return high, mid, (rest - mid.astype(f32)).astype(bf16)


def hot(mask):
    return jnp.where(mask, 1.0, 0.0).astype(bf16)


def rows_of(ref, group):
    return ref[pl.ds(pl.multiple_of(group * 8, 8), 8), :]


def put_rows(ref, group, rows):
    ref[pl.ds(pl.multiple_of(group * 8, 8), 8), :] = jnp.concatenate(rows, axis=0)


def to_slots(rs, sums):
    high, mid, low = thirds(sums)
    return dot(rs, high, NN) + dot(rs, mid, NN) + dot(rs, low, NN)


def prep_kernel(
    dev_ref, t_ref, av_ref, var_ref, mass_ref, bare_ref, par_ref, bp_ref, fp_ref, ri_ref, c_ref, sw_ref,
    e_out, mb_ref, rinv_ref, lab_ref, rs_ref, m_ref, sums_ref, edge_ref, count_ref, cols, weight_ref,
    pres, le, l1e, a1, b1, chi, arms, acc, e_ref, edge, sems,
):
    edge_ref[...] = edges_by_z(t_ref, edge)
    for s in range(SPEC):
        cols[s] = jnp.broadcast_to(c_ref[:, s : s + 1], (SPEC, ETA))
    weight_ref[...] = jnp.broadcast_to(
        jnp.sum(
            jnp.where(iota((SPEC, SPEC), 0) == iota((SPEC, SPEC), 1), sw_ref[...], 0.0), axis=1, keepdims=True
        ),
        (SPEC, ETA),
    )
    own = bp_ref[...] == dev_ref[0] * OWN + (iota((ROWS, SLOTS), 0) >> 4)
    count = jnp.sum(jnp.where(own, ri_ref[...] + 1, 0).astype(f32), axis=1, keepdims=True)
    count_ref[...] = jnp.broadcast_to(count, (ROWS, ETA))

    for block in range(4):
        ids = iota((128, 128), 0) + block * 128

        def seen(group, found):
            rows = rows_of(par_ref, group)
            for q in range(8):
                found = jnp.where(rows[q : q + 1] == ids, 1.0, found)
            return found

        found = lax.fori_loop(0, GROUPS, seen, jnp.zeros((128, 128), f32))
        pres[block * 128 : (block + 1) * 128, :] = found.astype(bf16)
    named = dot(pres[...], jnp.ones((128, 128), bf16), NN) > 0.5
    before = hot(iota((SLOTS, SLOTS), 1) < iota((SLOTS, SLOTS), 0))
    rank = dot(before, hot(named), NN)
    sel = hot(named & (rank == iota((SLOTS, 128), 1).astype(f32)))
    cell = iota((SLOTS, 128), 0) + 1
    upper = dot(sel, (cell >> 4).astype(f32).astype(bf16), TN)
    lower = dot(sel, (cell & 15).astype(f32).astype(bf16), TN)
    label = (upper * 16.0 + lower).astype(jnp.int32) - 1
    lab = label[:LABELS]
    lab_ref[...] = lab

    place = iota((SLOTS, SLOTS), 0)
    place = (place & 127) * OWN + (place >> 7)
    pt = hot(bp_ref[...] == place)
    rs = dot(pt, sel, NN).astype(bf16)[:, :LABELS]
    rs_ref[...] = rs
    other = iota((SLOTS, SLOTS), 0)
    adjacent = jnp.zeros((SLOTS, SLOTS), f32)
    for j in range(6):
        adjacent = adjacent + jnp.where(fp_ref[j : j + 1, :] == other, 1.0, 0.0)
    half = dot(pt, adjacent.astype(bf16), NT).astype(bf16)
    m_ref[...] = dot(half, pt, NT).astype(bf16)

    point = (iota((ETA, 128), 0).astype(f32) + 0.5) / ETA
    le[...] = jnp.log(point)
    l1e[...] = jnp.log(1.0 - point)
    shape_sum = 1.0 / var_ref[...] - 1.0
    a1[...] = av_ref[...] * shape_sum - 1.0
    b1[...] = (1.0 - av_ref[...]) * shape_sum - 1.0
    chi[...] = bare_ref[...] * (1.0 + 0.5 * jnp.tanh(t_ref[...]))
    acc[...] = jnp.zeros_like(acc)

    def tables(group, carry):
        a_rows, b_rows = rows_of(a1, group), rows_of(b1, group)
        chi_rows, mass_rows, par_rows = rows_of(chi, group), rows_of(mass_ref, group), rows_of(par_ref, group)
        inverse, mass_over = [], []
        for q in range(8):
            at = slice(q * 128, (q + 1) * 128)
            logits = a_rows[q : q + 1] * le[...] + b_rows[q : q + 1] * l1e[...]
            table = jnp.exp(logits - jnp.max(logits, axis=0, keepdims=True))
            r = 1.0 / jnp.sum(table, axis=0, keepdims=True)
            high, low = halves(table)
            e_ref[group, 0:128, at] = high
            e_ref[group, 128:256, at] = low
            w = mass_rows[q : q + 1] * r
            n = w * chi_rows[q : q + 1]
            inverse.append(r)
            mass_over.append(w)
            mine = lab == par_rows[q : q + 1]
            for k, part in enumerate((*halves(w), *halves(n))):
                arms[k * LABELS : (k + 1) * LABELS, at] = jnp.where(mine, part.astype(f32), 0.0).astype(bf16)
        put_rows(rinv_ref, group, inverse)
        put_rows(mb_ref, group, [jnp.concatenate(mass_over, axis=0) * rows_of(bare_ref, group)])
        pltpu.make_async_copy(e_ref.at[group], e_out.at[group], sems.at[group]).start()
        acc[...] += dot(arms[...], e_ref[group], NT)
        return carry

    lax.fori_loop(0, GROUPS, tables, 0)
    both = acc[:, :128] + acc[:, 128:]
    w48 = both[0:48] + both[48:96]
    n48 = both[96:144] + both[144:192]
    sums_ref[...] = to_slots(rs, jnp.concatenate([w48, n48], axis=1))
    for group in range(GROUPS):
        pltpu.make_async_copy(e_ref.at[group], e_out.at[group], sems.at[group]).wait()


def neighbour_sums(part, m):
    lane = iota((128, 128), 1)
    stacked = jnp.concatenate([jnp.where(lane >> 4 == t, part, 0.0) for t in range(OWN)], axis=0)
    high, low = halves(stacked)
    both = dot(m, jnp.concatenate([high, low], axis=1), NN)
    total = both[:, :128] + both[:, 128:]
    for shift in (64, 32, 16):
        total = total + pltpu.roll(total, shift, 1)
    out = jnp.zeros((128, 128), f32)
    for t in range(OWN):
        out = jnp.where(lane >> 4 == t, total[t * 128 : (t + 1) * 128], out)
    return out


def edges_by_z(t_ref, edge):
    edge[...] = jnp.zeros_like(edge)
    edge[64:80, :] = t_ref[0:16, :]
    edge[80:96, :] = t_ref[48:64, :]
    for x in range(4):
        edge[96 + x : 97 + x, :] = t_ref[16 * x : 16 * x + 1, :]
        edge[100 + x : 101 + x, :] = t_ref[16 * x + 15 : 16 * x + 16, :]
    return edge[...].T


def split_kernel(state_ref, out_ref):
    out_ref[...] = jnp.concatenate([state_ref[...], jnp.zeros((128 - ROWS, ETA), f32)], axis=0).T


def first_pack_kernel(got_ref, m_ref, sums_ref, edge_ref, out_ref):
    misc = neighbour_sums(got_ref[...], m_ref[...]) + edge_ref[...]
    for t in range(OWN):
        out_ref[pl.ds(t, 128, stride=FIRST), :] = sums_ref[t * 128 : (t + 1) * 128, 0:128]
        out_ref[pl.ds(OWN + t, 128, stride=FIRST), :] = sums_ref[t * 128 : (t + 1) * 128, 128:256]
    out_ref[pl.ds(2 * OWN, 128, stride=FIRST), :] = misc


def passed_on(misc):
    lane, row = iota((128, 128), 1), iota((128, 128), 0)
    gx, gy = row >> 3, row & 7
    out = jnp.where((lane >= 64) & (lane < 80) & (gx < 15), pltpu.roll(misc, 120, 0), 0.0)
    out = jnp.where((lane >= 80) & (lane < 96) & (gx > 0), pltpu.roll(misc, 8, 0), out)
    out = jnp.where((lane >= 96) & (lane < 100) & (gy < 7), pltpu.roll(misc, 127, 0), out)
    return jnp.where((lane >= 100) & (lane < 104) & (gy > 0), pltpu.roll(misc, 1, 0), out)


def advance(state_ref, misc, cchi, count_ref, cols, weight_ref, out_ref, last):
    count = count_ref[...]
    fraction = 1.0 / count
    mixing = fraction * mixing_rate * jnp.concatenate(
        [jnp.broadcast_to(cchi[t], (SPEC, ETA)) for t in range(OWN)], axis=0
    )
    reacting = fraction * react_rate
    near = misc.T[:ROWS]
    state = state_ref[...]
    state = state + coupling * (near - 6.0 * state)
    lane = iota((ROWS, ETA), 1)

    def substep(index, current):
        speed = jnp.tanh(current)
        source = []
        for t in range(OWN):
            parts = [speed[t * SPEC + s : t * SPEC + s + 1] * cols[s] for s in range(SPEC)]
            while len(parts) > 1:
                parts = [a + b for a, b in zip(parts[::2], parts[1::2])]
            source.append(parts[0])
        source = jnp.concatenate(source, axis=0)
        left = jnp.where(lane == 0, current, pltpu.roll(current, 1, 1))
        right = jnp.where(lane == ETA - 1, current, pltpu.roll(current, ETA - 1, 1))
        update = mixing * (right - 2.0 * current + left) + reacting * source
        return jnp.where(index.astype(f32) < count, current + update, current)

    state = lax.fori_loop(0, SUBMAX, substep, state)
    state_ref_out, pay = out_ref
    state_ref_out[...] = state
    weight = weight_ref[...]
    for t in range(OWN):
        theta = jnp.sum(weight * state[t * SPEC : (t + 1) * SPEC], axis=0, keepdims=True)
        pay[pl.ds(t, 128, stride=LATER), :] = jnp.broadcast_to(theta, (128, ETA))
    out = passed_on(misc)
    if not last:
        out = out + jnp.concatenate([state, jnp.zeros((128 - ROWS, ETA), f32)], axis=0).T
    pay[pl.ds(OWN, 128, stride=LATER), :] = out


def total_of(got_ref, row, stride):
    return jnp.sum(got_ref[pl.ds(row, 128, stride=stride), :], axis=0, keepdims=True)


def first_advance_kernel(
    got_ref, state_ref, count_ref, cols, weight_ref, state_out, weight_out, pay
):
    cchi = []
    for t in range(OWN):
        w = total_of(got_ref, t, FIRST)
        n = total_of(got_ref, OWN + t, FIRST)
        weight_out[t : t + 1, :] = w
        cchi.append((n + prior_flux) / (w + prior_weight))
    misc = got_ref[pl.ds(2 * OWN, 128, stride=FIRST), :]
    advance(state_ref, misc, cchi, count_ref, cols, weight_ref, (state_out, pay), False)


def later_advance_kernel(
    got_ref, state_ref, mass_ref, count_ref, cols, weight_ref, state_out, pay
):
    cchi = []
    for t in range(OWN):
        n = total_of(got_ref, t, LATER)
        cchi.append((n + prior_flux) / (mass_ref[t : t + 1, :] + prior_weight))
    misc = got_ref[pl.ds(OWN, 128, stride=LATER), :]
    advance(state_ref, misc, cchi, count_ref, cols, weight_ref, (state_out, pay), True)


def fine_update(got_ref, misc, t_ref, e_ref, rinv_ref, lab_ref, rs_ref, par_ref, tfine, grid):
    theta = jnp.concatenate([got_ref[pl.ds(t, 128, stride=LATER), :] for t in range(OWN)], axis=0)
    picked = dot(rs_ref[...], jnp.concatenate(halves(theta), axis=1), TN).astype(bf16)
    high, low = picked[:, :128], picked[:, 128:]
    rows = jnp.concatenate(
        [jnp.concatenate([high, high], axis=1), jnp.concatenate([low, low], axis=1)], axis=0
    )
    lab = lab_ref[...]

    def weigh(group, carry):
        means = dot(rows, e_ref[group], NN)
        means = means[:LABELS] + means[LABELS:]
        par_rows, inverse = rows_of(par_ref, group), rows_of(rinv_ref, group)
        out = []
        for q in range(8):
            mine = lab == par_rows[q : q + 1]
            out.append(jnp.sum(jnp.where(mine, means[:, q * 128 : (q + 1) * 128], 0.0), axis=0, keepdims=True))
        put_rows(tfine, group, [jnp.concatenate(out, axis=0) * inverse])
        return carry

    lax.fori_loop(0, GROUPS, weigh, 0)
    beside = misc.T
    t = t_ref[...]
    grid[1:5, 8:24, :] = t.reshape(4, 16, 128)
    grid[5, 8:24, :] = beside[64:80]
    grid[0, 8:24, :] = beside[80:96]
    for x in range(4):
        grid[1 + x, 24:25, :] = beside[96 + x : 97 + x]
        grid[1 + x, 7:8, :] = beside[100 + x : 101 + x]
    around = grid[2:6, 8:24, :] + grid[0:4, 8:24, :]
    around = around + grid[1:5, 9:25, :] + grid[1:5, 7:23, :]
    around = around.reshape(ROWS, 128)
    lane = iota((ROWS, 128), 1)
    around = around + jnp.where(lane == 127, 0.0, pltpu.roll(t, 127, 1))
    around = around + jnp.where(lane == 0, 0.0, pltpu.roll(t, 1, 1))
    return t + thermal_diffusion * (around - 6.0 * t) + damping_contribution * (tfine[...] - t)


def middle_kernel(
    got_ref, t_ref, e_ref, rinv_ref, mb_ref, lab_ref, rs_ref, m_ref, par_ref,
    t_out, pay, tfine, grid, flux, arms, acc, edge,
):
    misc = got_ref[pl.ds(OWN, 128, stride=LATER), :]
    t = fine_update(got_ref, misc, t_ref, e_ref, rinv_ref, lab_ref, rs_ref, par_ref, tfine, grid)
    t_out[...] = t
    flux[...] = mb_ref[...] * (1.0 + 0.5 * jnp.tanh(t))
    acc[...] = jnp.zeros_like(acc)
    lab = lab_ref[...]

    def gather(group, carry):
        flux_rows, par_rows = rows_of(flux, group), rows_of(par_ref, group)
        for q in range(8):
            mine = lab == par_rows[q : q + 1]
            for k, part in enumerate(halves(flux_rows[q : q + 1])):
                arms[k * LABELS : (k + 1) * LABELS, q * 128 : (q + 1) * 128] = jnp.where(
                    mine, part.astype(f32), 0.0
                ).astype(bf16)
        acc[...] += dot(arms[...], e_ref[group], NT)
        return carry

    lax.fori_loop(0, GROUPS, gather, 0)
    both = acc[:, :128] + acc[:, 128:]
    sums = to_slots(rs_ref[...], both[0:48] + both[48:96])
    for k in range(OWN):
        pay[pl.ds(k, 128, stride=LATER), :] = sums[k * 128 : (k + 1) * 128]
    out = neighbour_sums(misc, m_ref[...]) + edges_by_z(t_out, edge)
    pay[pl.ds(OWN, 128, stride=LATER), :] = out


def final_kernel(got_ref, t_ref, e_ref, rinv_ref, lab_ref, rs_ref, par_ref, t_out, tfine, grid):
    misc = got_ref[pl.ds(OWN, 128, stride=LATER), :]
    t_out[...] = fine_update(got_ref, misc, t_ref, e_ref, rinv_ref, lab_ref, rs_ref, par_ref, tfine, grid)


def call(kernel, outs, scratch, *operands, scalars=0, results=(), streamed=()):
    vmem, smem = pl.BlockSpec(memory_space=pltpu.VMEM), pl.BlockSpec(memory_space=pltpu.SMEM)
    away = set(results) | set(streamed)
    return pl.pallas_call(
        kernel,
        out_shape=[pltpu.HBM(*o) if i in away else pltpu.VMEM(*o) for i, o in enumerate(outs)],
        in_specs=[smem] * scalars + [vmem] * (len(operands) - scalars),
        out_specs=[pl.BlockSpec(memory_space=pl.ANY) if i in streamed else vmem for i in range(len(outs))],
        scratch_shapes=[pltpu.VMEM(*s) if isinstance(s, tuple) else s for s in scratch],
        compiler_params=pltpu.CompilerParams(vmem_limit_bytes=24 << 20),
    )(*operands)


def exchange(array):
    rows = array.shape[0] // DEV
    sent = array.reshape(DEV, 1, rows * 128)
    return lax.all_to_all(sent, ("gx", "gy"), 0, 0, tiled=True).reshape(array.shape)


def from_hbm(*arrays):
    return [pltpu.with_memory_space_constraint(a, pltpu.HBM) for a in arrays]


def shards(thermal, average, variance, mass, bare, parent, species, position, partners, increments, chem, weight):
    dev = (lax.axis_index("gx") * 8 + lax.axis_index("gy")).astype(jnp.int32).reshape(1)
    fine = [a.reshape(ROWS, 128) for a in (thermal, average, variance, mass, bare, parent)]
    t0, av, var, mass, bare, par = fine
    state = species.reshape(ROWS, ETA)
    bp, ri, sw = position.reshape(1, SLOTS), increments.reshape(1, SLOTS), weight.reshape(1, SPEC)
    cells = ((ROWS, 128), f32)
    square = ((128, 128), f32)
    pay = ((DEV * LATER, 128), f32)

    states = exchange(call(split_kernel, [square], [], *from_hbm(state))[0])
    table, mb, rinv, lab, rs, m, sums, edges, count, cols, sw = call(
        prep_kernel,
        [((GROUPS, 256, WIDE), bf16), cells, cells, ((LABELS, 128), jnp.int32), ((SLOTS, LABELS), bf16),
         ((SLOTS, SLOTS), bf16), ((SLOTS, 256), f32), square, cells, ((SPEC, SPEC, ETA), f32), ((SPEC, ETA), f32)],
        [((SLOTS, 128), bf16), square, square, cells, cells, cells, ((4 * LABELS, WIDE), bf16),
         ((4 * LABELS, 256), f32), ((GROUPS, 256, WIDE), bf16), square, pltpu.SemaphoreType.DMA((GROUPS,))],
        dev, *from_hbm(t0, av, var, mass, bare, par, bp, partners.T, ri, chem, sw), scalars=1, streamed=(0,),
    )
    (sent,) = call(first_pack_kernel, [((DEV * FIRST, 128), f32)], [], states, m, sums, edges)
    got = exchange(sent)
    state, own_weight, sent = call(
        first_advance_kernel, [((ROWS, ETA), f32), ((8, 128), f32), pay], [],
        got, *from_hbm(state), count, cols, sw,
    )
    got = exchange(sent)
    grid = ((6, 32, 128), f32)
    t1, sent = call(
        middle_kernel, [cells, pay],
        [cells, grid, cells, ((2 * LABELS, WIDE), bf16), ((2 * LABELS, 256), f32), square],
        got, t0, table, rinv, mb, lab, rs, m, par,
    )
    got = exchange(sent)
    state, sent = call(
        later_advance_kernel, [((ROWS, ETA), f32), pay], [],
        got, state, own_weight, count, cols, sw, results=(0,),
    )
    got = exchange(sent)
    (t2,) = call(final_kernel, [cells], [cells, grid], got, t1, table, rinv, lab, rs, par, results=(0,))
    return state.reshape(species.shape), t2.reshape(thermal.shape)


def solution(mesh):
    fine = P("gx", "gy", None)
    slots = P(("gx", "gy"), None, None)
    return jax.shard_map(
        shards,
        mesh=mesh,
        in_specs=(fine,) * 6 + (slots,) + (P(),) * 5,
        out_specs=(slots, fine),
        check_vma=False,
    )
```

```python
import jax
import jax.numpy as jnp
from jax import lax
from jax.experimental import pallas as pl
from jax.experimental.pallas import tpu as pltpu
from jax.sharding import PartitionSpec as P

DEV = 128
OWN = 4
SLOTS = 512
SPEC = 16
ETA = 128
ROWS = 64
SUBMAX = 16
LABELS = 48
GROUPS = 8
WIDE = 1024
FIRST = 9
LATER = 5
UNROLL = 4
LOG2E = 1.4426950408889634

coupling = 0.05
mixing_rate = 0.2
react_rate = 0.5
prior_weight = 1.0
prior_flux = 0.5
thermal_diffusion = 0.1
damping_contribution = 0.3

f32 = jnp.float32
bf16 = jnp.bfloat16
NN = ((1,), (0,))
NT = ((1,), (1,))
TN = ((0,), (0,))


def dot(a, b, dims):
    return lax.dot_general(a, b, (dims, ((), ())), preferred_element_type=f32)


def iota(shape, dim):
    return lax.broadcasted_iota(jnp.int32, shape, dim)


def halves(x):
    high = x.astype(bf16)
    return high, (x - high.astype(f32)).astype(bf16)


def thirds(x):
    high = x.astype(bf16)
    rest = x - high.astype(f32)
    mid = rest.astype(bf16)
    return high, mid, (rest - mid.astype(f32)).astype(bf16)


def hot(mask):
    return jnp.where(mask, 1.0, 0.0).astype(bf16)


def marked(mask):
    return jnp.where(mask, jnp.ones((), bf16), jnp.zeros((), bf16))


def rows_of(ref, group):
    return ref[pl.ds(pl.multiple_of(group * 8, 8), 8), :]


def put_rows(ref, group, rows):
    ref[pl.ds(pl.multiple_of(group * 8, 8), 8), :] = jnp.concatenate(rows, axis=0)


def to_slots(rs, sums):
    high, mid, low = thirds(sums)
    return dot(rs, high, NN) + dot(rs, mid, NN) + dot(rs, low, NN)


def prep_kernel(
    dev_ref, t_ref, av_ref, var_ref, mass_ref, bare_ref, par_ref, bp_ref, fp_ref, ri_ref, c_ref, sw_ref,
    e_out, mb_ref, rinv_ref, lab_ref, rs_ref, m_ref, sums_ref, edge_ref, count_ref, cols, weight_ref, who_ref,
    le, l1e, a1, b1, chi, arms, acc, e_ref, edge, sems,
):
    edge_ref[...] = edges_by_z(t_ref, edge)
    for s in range(SPEC):
        cols[s] = jnp.broadcast_to(c_ref[:, s : s + 1], (SPEC, ETA))
    weight_ref[...] = jnp.broadcast_to(
        jnp.sum(
            jnp.where(iota((SPEC, SPEC), 0) == iota((SPEC, SPEC), 1), sw_ref[...], 0.0), axis=1, keepdims=True
        ),
        (SPEC, ETA),
    )
    own = bp_ref[...] == dev_ref[0] * OWN + (iota((ROWS, SLOTS), 0) >> 4)
    count = jnp.sum(jnp.where(own, ri_ref[...] + 1, 0).astype(f32), axis=1, keepdims=True)
    count_ref[...] = jnp.broadcast_to(count, (ROWS, ETA))

    named = jnp.zeros((32, 16), f32)
    for group in range(GROUPS):
        rows = par_ref[group * 8 : (group + 1) * 8, :]
        tall, short = rows >> 4, rows & 15
        tall = jnp.concatenate([hot(tall[q : q + 1] == iota((32, 128), 0)) for q in range(8)], axis=1)
        short = jnp.concatenate([hot(short[q : q + 1] == iota((16, 128), 0)) for q in range(8)], axis=1)
        named = named + dot(tall, short, NT)
    named = hot(named > 0.5)
    within = dot(named, hot(iota((16, 16), 0) < iota((16, 16), 1)), NN)
    ahead = dot(hot(iota((32, 32), 1) < iota((32, 32), 0)), named, NN).astype(bf16)
    ahead = dot(ahead, jnp.ones((16, 16), bf16), NN)
    order = jnp.where(named > 0, within + ahead + 1.0, 0.0).astype(bf16)
    spread = dot(hot(iota((SLOTS, 32), 0) >> 4 == iota((SLOTS, 32), 1)), order, NN)
    spread = jnp.where(iota((SLOTS, 16), 0) & 15 == iota((SLOTS, 16), 1), spread, 0.0).astype(bf16)
    order = dot(spread, jnp.ones((16, 128), bf16), NN)
    sel = hot(order == (iota((SLOTS, 128), 1) + 1).astype(f32))
    cell = iota((SLOTS, 128), 0) + 1
    label = dot(
        sel,
        jnp.concatenate([(cell >> 4).astype(f32).astype(bf16), (cell & 15).astype(f32).astype(bf16)], axis=1),
        TN,
    )
    lab = ((label[:, :128] * 16.0 + label[:, 128:]).astype(jnp.int32) - 1)[:LABELS]
    lab_ref[...] = lab

    bp = bp_ref[...]
    device = iota((128, SLOTS), 0).astype(f32).astype(bf16)
    pt = jnp.concatenate(
        [
            marked(jnp.where(bp & 3 == t, bp >> 2, -1).astype(f32).astype(bf16) == device)
            for t in range(OWN)
        ],
        axis=0,
    )
    rs = dot(pt, sel, NN).astype(bf16)[:, :LABELS]
    rs_ref[...] = rs
    other = iota((256, SLOTS), 0).astype(f32).astype(bf16)
    near = fp_ref[...]
    adjacent = []
    for half in range(2):
        part = near - 256 * half
        part = jnp.where((part >= 0) & (part < 256), part, -1).astype(f32)
        total = jnp.zeros((256, SLOTS), bf16)
        for j in range(6):
            total = total + marked(part[j : j + 1].astype(bf16) == other)
        adjacent.append(total)
    half = dot(pt, jnp.concatenate(adjacent, axis=0), NT).astype(bf16)
    m_ref[...] = dot(half, pt, NT).astype(bf16)

    point = (iota((ETA, 128), 0).astype(f32) + 0.5) / ETA
    le[...] = jnp.log(point) * LOG2E
    l1e[...] = jnp.log(1.0 - point) * LOG2E
    shape_sum = 1.0 / var_ref[...] - 1.0
    a1[...] = av_ref[...] * shape_sum - 1.0
    b1[...] = (1.0 - av_ref[...]) * shape_sum - 1.0
    chi[...] = bare_ref[...] * (1.0 + 0.5 * jnp.tanh(t_ref[...]))
    acc[...] = jnp.zeros_like(acc)

    def tables(group, carry):
        a_rows, b_rows = rows_of(a1, group), rows_of(b1, group)
        chi_rows, mass_rows, par_rows = rows_of(chi, group), rows_of(mass_ref, group), rows_of(par_ref, group)
        inverse, mass_over = [], []
        for q in range(8):
            at = slice(q * 128, (q + 1) * 128)
            logits = a_rows[q : q + 1] * le[...] + b_rows[q : q + 1] * l1e[...]
            table = jnp.exp2(logits - jnp.max(logits, axis=0, keepdims=True))
            r = 1.0 / jnp.sum(table, axis=0, keepdims=True)
            high, low = halves(table)
            e_ref[group, 0:128, at] = high
            e_ref[group, 128:256, at] = low
            w = mass_rows[q : q + 1] * r
            n = w * chi_rows[q : q + 1]
            inverse.append(r)
            mass_over.append(w)
            mine = hot(lab == par_rows[q : q + 1])
            who_ref[group, :, at] = mine
            for k, part in enumerate((*halves(w), *halves(n))):
                arms[k * LABELS : (k + 1) * LABELS, at] = mine * part
        put_rows(rinv_ref, group, inverse)
        put_rows(mb_ref, group, [jnp.concatenate(mass_over, axis=0) * rows_of(bare_ref, group)])
        pltpu.make_async_copy(e_ref.at[group], e_out.at[group], sems.at[group]).start()
        acc[...] += dot(arms[...], e_ref[group, 0:128], NT)
        return carry

    lax.fori_loop(0, GROUPS, tables, 0, unroll=UNROLL)
    both = acc[...]
    w48 = both[0:48] + both[48:96]
    n48 = both[96:144] + both[144:192]
    sums_ref[...] = to_slots(rs, jnp.concatenate([w48, n48], axis=1))
    for group in range(GROUPS):
        pltpu.make_async_copy(e_ref.at[group], e_out.at[group], sems.at[group]).wait()


def neighbour_sums(part, m):
    lane = iota((128, 128), 1)
    stacked = jnp.concatenate([jnp.where(lane >> 4 == t, part, 0.0) for t in range(OWN)], axis=0)
    high, low = halves(stacked)
    both = dot(m, jnp.concatenate([high, low], axis=1), NN)
    total = both[:, :128] + both[:, 128:]
    for shift in (64, 32, 16):
        total = total + pltpu.roll(total, shift, 1)
    out = jnp.zeros((128, 128), f32)
    for t in range(OWN):
        out = jnp.where(lane >> 4 == t, total[t * 128 : (t + 1) * 128], out)
    return out


def edges_by_z(t_ref, edge):
    edge[...] = jnp.zeros_like(edge)
    edge[64:80, :] = t_ref[0:16, :]
    edge[80:96, :] = t_ref[48:64, :]
    for x in range(4):
        edge[96 + x : 97 + x, :] = t_ref[16 * x : 16 * x + 1, :]
        edge[100 + x : 101 + x, :] = t_ref[16 * x + 15 : 16 * x + 16, :]
    return edge[...].T


def split_kernel(state_ref, out_ref):
    out_ref[...] = jnp.concatenate([state_ref[...], jnp.zeros((128 - ROWS, ETA), f32)], axis=0).T


def first_pack_kernel(got_ref, m_ref, sums_ref, edge_ref, out_ref):
    misc = neighbour_sums(got_ref[...], m_ref[...]) + edge_ref[...]
    for t in range(OWN):
        out_ref[pl.ds(t, 128, stride=FIRST), :] = sums_ref[t * 128 : (t + 1) * 128, 0:128]
        out_ref[pl.ds(OWN + t, 128, stride=FIRST), :] = sums_ref[t * 128 : (t + 1) * 128, 128:256]
    out_ref[pl.ds(2 * OWN, 128, stride=FIRST), :] = misc


def passed_on(misc):
    lane, row = iota((128, 128), 1), iota((128, 128), 0)
    gx, gy = row >> 3, row & 7
    out = jnp.where((lane >= 64) & (lane < 80) & (gx < 15), pltpu.roll(misc, 120, 0), 0.0)
    out = jnp.where((lane >= 80) & (lane < 96) & (gx > 0), pltpu.roll(misc, 8, 0), out)
    out = jnp.where((lane >= 96) & (lane < 100) & (gy < 7), pltpu.roll(misc, 127, 0), out)
    return jnp.where((lane >= 100) & (lane < 104) & (gy > 0), pltpu.roll(misc, 1, 0), out)


def advance(state_ref, misc, cchi, count_ref, cols, weight_ref, out_ref, last):
    count = count_ref[...]
    fraction = 1.0 / count
    mixing = fraction * mixing_rate * jnp.concatenate(
        [jnp.broadcast_to(cchi[t], (SPEC, ETA)) for t in range(OWN)], axis=0
    )
    reacting = fraction * react_rate
    near = misc.T[:ROWS]
    state = state_ref[...]
    state = state + coupling * (near - 6.0 * state)
    lane = iota((ROWS, ETA), 1)

    def substep(index, current):
        speed = jnp.tanh(current)
        source = []
        for t in range(OWN):
            parts = [speed[t * SPEC + s : t * SPEC + s + 1] * cols[s] for s in range(SPEC)]
            while len(parts) > 1:
                parts = [a + b for a, b in zip(parts[::2], parts[1::2])]
            source.append(parts[0])
        source = jnp.concatenate(source, axis=0)
        left = jnp.where(lane == 0, current, pltpu.roll(current, 1, 1))
        right = jnp.where(lane == ETA - 1, current, pltpu.roll(current, ETA - 1, 1))
        update = mixing * (right - 2.0 * current + left) + reacting * source
        return jnp.where(index.astype(f32) < count, current + update, current)

    state = lax.fori_loop(0, SUBMAX, substep, state)
    state_ref_out, pay = out_ref
    state_ref_out[...] = state
    weight = weight_ref[...]
    for t in range(OWN):
        theta = jnp.sum(weight * state[t * SPEC : (t + 1) * SPEC], axis=0, keepdims=True)
        pay[pl.ds(t, 128, stride=LATER), :] = jnp.broadcast_to(theta, (128, ETA))
    out = passed_on(misc)
    if not last:
        out = out + jnp.concatenate([state, jnp.zeros((128 - ROWS, ETA), f32)], axis=0).T
    pay[pl.ds(OWN, 128, stride=LATER), :] = out


def total_of(got_ref, row, stride):
    return jnp.sum(got_ref[pl.ds(row, 128, stride=stride), :], axis=0, keepdims=True)


def first_advance_kernel(
    got_ref, state_ref, count_ref, cols, weight_ref, state_out, weight_out, pay
):
    cchi = []
    for t in range(OWN):
        w = total_of(got_ref, t, FIRST)
        n = total_of(got_ref, OWN + t, FIRST)
        weight_out[t : t + 1, :] = w
        cchi.append((n + prior_flux) / (w + prior_weight))
    misc = got_ref[pl.ds(2 * OWN, 128, stride=FIRST), :]
    advance(state_ref, misc, cchi, count_ref, cols, weight_ref, (state_out, pay), False)


def later_advance_kernel(
    got_ref, state_ref, mass_ref, count_ref, cols, weight_ref, state_out, pay
):
    cchi = []
    for t in range(OWN):
        n = total_of(got_ref, t, LATER)
        cchi.append((n + prior_flux) / (mass_ref[t : t + 1, :] + prior_weight))
    misc = got_ref[pl.ds(OWN, 128, stride=LATER), :]
    advance(state_ref, misc, cchi, count_ref, cols, weight_ref, (state_out, pay), True)


def fine_update(got_ref, misc, t_ref, e_ref, rinv_ref, lab_ref, rs_ref, par_ref, tfine, grid):
    theta = jnp.concatenate([got_ref[pl.ds(t, 128, stride=LATER), :] for t in range(OWN)], axis=0)
    picked = dot(rs_ref[...], jnp.concatenate(halves(theta), axis=1), TN).astype(bf16)
    high, low = picked[:, :128], picked[:, 128:]
    rows = jnp.concatenate(
        [jnp.concatenate([high, high], axis=1), jnp.concatenate([low, low], axis=1)], axis=0
    )
    lab = lab_ref[...]

    def weigh(group, carry):
        means = dot(rows, e_ref[group], NN)
        means = means[:LABELS] + means[LABELS:]
        par_rows, inverse = rows_of(par_ref, group), rows_of(rinv_ref, group)
        out = []
        for q in range(8):
            mine = lab == par_rows[q : q + 1]
            out.append(jnp.sum(jnp.where(mine, means[:, q * 128 : (q + 1) * 128], 0.0), axis=0, keepdims=True))
        put_rows(tfine, group, [jnp.concatenate(out, axis=0) * inverse])
        return carry

    lax.fori_loop(0, GROUPS, weigh, 0, unroll=UNROLL)
    beside = misc.T
    t = t_ref[...]
    grid[1:5, 8:24, :] = t.reshape(4, 16, 128)
    grid[5, 8:24, :] = beside[64:80]
    grid[0, 8:24, :] = beside[80:96]
    for x in range(4):
        grid[1 + x, 24:25, :] = beside[96 + x : 97 + x]
        grid[1 + x, 7:8, :] = beside[100 + x : 101 + x]
    around = grid[2:6, 8:24, :] + grid[0:4, 8:24, :]
    around = around + grid[1:5, 9:25, :] + grid[1:5, 7:23, :]
    around = around.reshape(ROWS, 128)
    lane = iota((ROWS, 128), 1)
    around = around + jnp.where(lane == 127, 0.0, pltpu.roll(t, 127, 1))
    around = around + jnp.where(lane == 0, 0.0, pltpu.roll(t, 1, 1))
    return t + thermal_diffusion * (around - 6.0 * t) + damping_contribution * (tfine[...] - t)


def middle_kernel(
    got_ref, t_ref, e_ref, rinv_ref, mb_ref, lab_ref, rs_ref, m_ref, par_ref, who_ref,
    t_out, pay, tfine, grid, flux, arms, acc, edge,
):
    misc = got_ref[pl.ds(OWN, 128, stride=LATER), :]
    t = fine_update(got_ref, misc, t_ref, e_ref, rinv_ref, lab_ref, rs_ref, par_ref, tfine, grid)
    t_out[...] = t
    flux[...] = mb_ref[...] * (1.0 + 0.5 * jnp.tanh(t))
    acc[...] = jnp.zeros_like(acc)

    def gather(group, carry):
        flux_rows = rows_of(flux, group)
        for q in range(8):
            at = slice(q * 128, (q + 1) * 128)
            for k, part in enumerate(halves(flux_rows[q : q + 1])):
                arms[k * LABELS : (k + 1) * LABELS, at] = who_ref[group, :, at] * part
        acc[...] += dot(arms[...], e_ref[group, 0:128], NT)
        return carry

    lax.fori_loop(0, GROUPS, gather, 0, unroll=UNROLL)
    both = acc[...]
    sums = to_slots(rs_ref[...], both[0:48] + both[48:96])
    for k in range(OWN):
        pay[pl.ds(k, 128, stride=LATER), :] = sums[k * 128 : (k + 1) * 128]
    out = neighbour_sums(misc, m_ref[...]) + edges_by_z(t_out, edge)
    pay[pl.ds(OWN, 128, stride=LATER), :] = out


def final_kernel(got_ref, t_ref, e_ref, rinv_ref, lab_ref, rs_ref, par_ref, t_out, tfine, grid):
    misc = got_ref[pl.ds(OWN, 128, stride=LATER), :]
    t_out[...] = fine_update(got_ref, misc, t_ref, e_ref, rinv_ref, lab_ref, rs_ref, par_ref, tfine, grid)


def call(kernel, outs, scratch, *operands, scalars=0, results=(), streamed=()):
    vmem, smem = pl.BlockSpec(memory_space=pltpu.VMEM), pl.BlockSpec(memory_space=pltpu.SMEM)
    away = set(results) | set(streamed)
    return pl.pallas_call(
        kernel,
        out_shape=[pltpu.HBM(*o) if i in away else pltpu.VMEM(*o) for i, o in enumerate(outs)],
        in_specs=[smem] * scalars + [vmem] * (len(operands) - scalars),
        out_specs=[pl.BlockSpec(memory_space=pl.ANY) if i in streamed else vmem for i in range(len(outs))],
        scratch_shapes=[pltpu.VMEM(*s) if isinstance(s, tuple) else s for s in scratch],
        compiler_params=pltpu.CompilerParams(vmem_limit_bytes=24 << 20),
    )(*operands)


def exchange(array):
    rows = array.shape[0] // DEV
    sent = array.reshape(DEV, 1, rows * 128)
    return lax.all_to_all(sent, ("gx", "gy"), 0, 0, tiled=True).reshape(array.shape)


def from_hbm(*arrays):
    return [pltpu.with_memory_space_constraint(a, pltpu.HBM) for a in arrays]


def shards(thermal, average, variance, mass, bare, parent, species, position, partners, increments, chem, weight):
    dev = (lax.axis_index("gx") * 8 + lax.axis_index("gy")).astype(jnp.int32).reshape(1)
    fine = [a.reshape(ROWS, 128) for a in (thermal, average, variance, mass, bare, parent)]
    t0, av, var, mass, bare, par = fine
    state = species.reshape(ROWS, ETA)
    bp, ri, sw = position.reshape(1, SLOTS), increments.reshape(1, SLOTS), weight.reshape(1, SPEC)
    cells = ((ROWS, 128), f32)
    square = ((128, 128), f32)
    pay = ((DEV * LATER, 128), f32)

    states = exchange(call(split_kernel, [square], [], *from_hbm(state))[0])
    table, mb, rinv, lab, rs, m, sums, edges, count, cols, sw, who = call(
        prep_kernel,
        [((GROUPS, 256, WIDE), bf16), cells, cells, ((LABELS, 128), jnp.int32), ((SLOTS, LABELS), bf16),
         ((SLOTS, SLOTS), bf16), ((SLOTS, 256), f32), square, cells, ((SPEC, SPEC, ETA), f32), ((SPEC, ETA), f32),
         ((GROUPS, LABELS, WIDE), bf16)],
        [square, square, cells, cells, cells, ((4 * LABELS, WIDE), bf16),
         ((4 * LABELS, 128), f32), ((GROUPS, 256, WIDE), bf16), square, pltpu.SemaphoreType.DMA((GROUPS,))],
        dev, *from_hbm(t0, av, var, mass, bare, par, bp, partners.T, ri, chem, sw), scalars=1, streamed=(0,),
    )
    (sent,) = call(first_pack_kernel, [((DEV * FIRST, 128), f32)], [], states, m, sums, edges)
    got = exchange(sent)
    state, own_weight, sent = call(
        first_advance_kernel, [((ROWS, ETA), f32), ((8, 128), f32), pay], [],
        got, *from_hbm(state), count, cols, sw,
    )
    got = exchange(sent)
    grid = ((6, 32, 128), f32)
    t1, sent = call(
        middle_kernel, [cells, pay],
        [cells, grid, cells, ((2 * LABELS, WIDE), bf16), ((2 * LABELS, 128), f32), square],
        got, t0, table, rinv, mb, lab, rs, m, par, who,
    )
    got = exchange(sent)
    state, sent = call(
        later_advance_kernel, [((ROWS, ETA), f32), pay], [],
        got, state, own_weight, count, cols, sw, results=(0,),
    )
    got = exchange(sent)
    (t2,) = call(final_kernel, [cells], [cells, grid], got, t1, table, rinv, lab, rs, par, results=(0,))
    return state.reshape(species.shape), t2.reshape(thermal.shape)


def solution(mesh):
    fine = P("gx", "gy", None)
    slots = P(("gx", "gy"), None, None)
    return jax.shard_map(
        shards,
        mesh=mesh,
        in_specs=(fine,) * 6 + (slots,) + (P(),) * 5,
        out_specs=(slots, fine),
        check_vma=False,
    )
```

```python
import jax
import jax.numpy as jnp
from jax import lax
from jax.experimental import pallas as pl
from jax.experimental.pallas import tpu as pltpu
from jax.sharding import PartitionSpec as P

DEV = 128
OWN = 4
SLOTS = 512
SPEC = 16
ETA = 128
ROWS = 64
SUBMAX = 16
LABELS = 48
GROUPS = 8
WIDE = 1024
FIRST = 9
LATER = 5
UNROLL = 8
LOG2E = 1.4426950408889634

coupling = 0.05
mixing_rate = 0.2
react_rate = 0.5
prior_weight = 1.0
prior_flux = 0.5
thermal_diffusion = 0.1
damping_contribution = 0.3

f32 = jnp.float32
bf16 = jnp.bfloat16
NN = ((1,), (0,))
NT = ((1,), (1,))
TN = ((0,), (0,))


def dot(a, b, dims):
    return lax.dot_general(a, b, (dims, ((), ())), preferred_element_type=f32)


def iota(shape, dim):
    return lax.broadcasted_iota(jnp.int32, shape, dim)


def halves(x):
    high = x.astype(bf16)
    return high, (x - high.astype(f32)).astype(bf16)


def thirds(x):
    high = x.astype(bf16)
    rest = x - high.astype(f32)
    mid = rest.astype(bf16)
    return high, mid, (rest - mid.astype(f32)).astype(bf16)


def hot(mask):
    return jnp.where(mask, 1.0, 0.0).astype(bf16)


def marked(mask):
    return jnp.where(mask, jnp.ones((), bf16), jnp.zeros((), bf16))


def rows_of(ref, group):
    return ref[pl.ds(pl.multiple_of(group * 8, 8), 8), :]


def put_rows(ref, group, rows):
    ref[pl.ds(pl.multiple_of(group * 8, 8), 8), :] = jnp.concatenate(rows, axis=0)


def to_slots(rs, sums):
    high, mid, low = thirds(sums)
    return dot(rs, high, NN) + dot(rs, mid, NN) + dot(rs, low, NN)


def prep_kernel(
    dev_ref, t_ref, av_ref, var_ref, mass_ref, bare_ref, par_ref, bp_ref, fp_ref, ri_ref, c_ref, sw_ref,
    e_out, mb_ref, rinv_ref, lab_ref, rs_ref, m_ref, sums_ref, edge_ref, count_ref, cols, weight_ref, who_ref,
    le, l1e, a1, b1, chi, arms, acc, e_ref, edge, sems,
):
    edge_ref[...] = edges_by_z(t_ref, edge)
    for s in range(SPEC):
        cols[s] = jnp.broadcast_to(c_ref[:, s : s + 1], (SPEC, ETA))
    weight_ref[...] = jnp.broadcast_to(
        jnp.sum(
            jnp.where(iota((SPEC, SPEC), 0) == iota((SPEC, SPEC), 1), sw_ref[...], 0.0), axis=1, keepdims=True
        ),
        (SPEC, ETA),
    )
    own = bp_ref[...] == dev_ref[0] * OWN + (iota((ROWS, SLOTS), 0) >> 4)
    count = jnp.sum(jnp.where(own, ri_ref[...] + 1, 0).astype(f32), axis=1, keepdims=True)
    count_ref[...] = jnp.broadcast_to(count, (ROWS, ETA))

    named = jnp.zeros((32, 16), f32)
    for group in range(GROUPS):
        rows = par_ref[group * 8 : (group + 1) * 8, :]
        tall, short = rows >> 4, rows & 15
        tall = jnp.concatenate([hot(tall[q : q + 1] == iota((32, 128), 0)) for q in range(8)], axis=1)
        short = jnp.concatenate([hot(short[q : q + 1] == iota((16, 128), 0)) for q in range(8)], axis=1)
        named = named + dot(tall, short, NT)
    named = hot(named > 0.5)
    within = dot(named, hot(iota((16, 16), 0) < iota((16, 16), 1)), NN)
    ahead = dot(hot(iota((32, 32), 1) < iota((32, 32), 0)), named, NN).astype(bf16)
    ahead = dot(ahead, jnp.ones((16, 16), bf16), NN)
    order = jnp.where(named > 0, within + ahead + 1.0, 0.0).astype(bf16)
    spread = dot(hot(iota((SLOTS, 32), 0) >> 4 == iota((SLOTS, 32), 1)), order, NN)
    spread = jnp.where(iota((SLOTS, 16), 0) & 15 == iota((SLOTS, 16), 1), spread, 0.0).astype(bf16)
    order = dot(spread, jnp.ones((16, 128), bf16), NN)
    sel = hot(order == (iota((SLOTS, 128), 1) + 1).astype(f32))
    cell = iota((SLOTS, 128), 0) + 1
    label = dot(
        sel,
        jnp.concatenate([(cell >> 4).astype(f32).astype(bf16), (cell & 15).astype(f32).astype(bf16)], axis=1),
        TN,
    )
    lab = ((label[:, :128] * 16.0 + label[:, 128:]).astype(jnp.int32) - 1)[:LABELS]
    lab_ref[...] = lab

    bp = bp_ref[...]
    device = iota((128, SLOTS), 0).astype(f32).astype(bf16)
    pt = jnp.concatenate(
        [
            marked(jnp.where(bp & 3 == t, bp >> 2, -1).astype(f32).astype(bf16) == device)
            for t in range(OWN)
        ],
        axis=0,
    )
    rs = dot(pt, sel, NN).astype(bf16)[:, :LABELS]
    rs_ref[...] = rs
    other = iota((256, SLOTS), 0).astype(f32).astype(bf16)
    near = fp_ref[...]
    adjacent = []
    for half in range(2):
        part = near - 256 * half
        part = jnp.where((part >= 0) & (part < 256), part, -1).astype(f32)
        total = jnp.zeros((256, SLOTS), bf16)
        for j in range(6):
            total = total + marked(part[j : j + 1].astype(bf16) == other)
        adjacent.append(total)
    half = dot(pt, jnp.concatenate(adjacent, axis=0), NT).astype(bf16)
    m_ref[...] = dot(half, pt, NT).astype(bf16)

    point = (iota((ETA, 128), 0).astype(f32) + 0.5) / ETA
    le[...] = jnp.log(point) * LOG2E
    l1e[...] = jnp.log(1.0 - point) * LOG2E
    shape_sum = 1.0 / var_ref[...] - 1.0
    a1[...] = av_ref[...] * shape_sum - 1.0
    b1[...] = (1.0 - av_ref[...]) * shape_sum - 1.0
    chi[...] = bare_ref[...] * (1.0 + 0.5 * jnp.tanh(t_ref[...]))
    acc[...] = jnp.zeros_like(acc)

    def tables(group, carry):
        a_rows, b_rows = rows_of(a1, group), rows_of(b1, group)
        chi_rows, mass_rows, par_rows = rows_of(chi, group), rows_of(mass_ref, group), rows_of(par_ref, group)
        inverse, mass_over = [], []
        for q in range(8):
            at = slice(q * 128, (q + 1) * 128)
            logits = a_rows[q : q + 1] * le[...] + b_rows[q : q + 1] * l1e[...]
            table = jnp.exp2(logits - jnp.max(logits, axis=0, keepdims=True))
            r = 1.0 / jnp.sum(table, axis=0, keepdims=True)
            high, low = halves(table)
            e_ref[group, 0:128, at] = high
            e_ref[group, 128:256, at] = low
            w = mass_rows[q : q + 1] * r
            n = w * chi_rows[q : q + 1]
            inverse.append(r)
            mass_over.append(w)
            mine = hot(lab == par_rows[q : q + 1])
            who_ref[group, :, at] = mine
            for k, part in enumerate((*halves(w), *halves(n))):
                arms[k * LABELS : (k + 1) * LABELS, at] = mine * part
        put_rows(rinv_ref, group, inverse)
        put_rows(mb_ref, group, [jnp.concatenate(mass_over, axis=0) * rows_of(bare_ref, group)])
        pltpu.make_async_copy(e_ref.at[group], e_out.at[group], sems.at[group]).start()
        acc[...] += dot(arms[...], e_ref[group, 0:128], NT)
        return carry

    lax.fori_loop(0, GROUPS, tables, 0, unroll=UNROLL)
    both = acc[...]
    w48 = both[0:48] + both[48:96]
    n48 = both[96:144] + both[144:192]
    sums_ref[...] = to_slots(rs, jnp.concatenate([w48, n48], axis=1))
    for group in range(GROUPS):
        pltpu.make_async_copy(e_ref.at[group], e_out.at[group], sems.at[group]).wait()


def neighbour_sums(part, m):
    lane = iota((128, 128), 1)
    stacked = jnp.concatenate([jnp.where(lane >> 4 == t, part, 0.0) for t in range(OWN)], axis=0)
    high, low = halves(stacked)
    both = dot(m, jnp.concatenate([high, low], axis=1), NN)
    total = both[:, :128] + both[:, 128:]
    for shift in (64, 32, 16):
        total = total + pltpu.roll(total, shift, 1)
    out = jnp.zeros((128, 128), f32)
    for t in range(OWN):
        out = jnp.where(lane >> 4 == t, total[t * 128 : (t + 1) * 128], out)
    return out


def edges_by_z(t_ref, edge):
    edge[...] = jnp.zeros_like(edge)
    edge[64:80, :] = t_ref[0:16, :]
    edge[80:96, :] = t_ref[48:64, :]
    for x in range(4):
        edge[96 + x : 97 + x, :] = t_ref[16 * x : 16 * x + 1, :]
        edge[100 + x : 101 + x, :] = t_ref[16 * x + 15 : 16 * x + 16, :]
    return edge[...].T


def first_pack_kernel(got_ref, m_ref, sums_ref, edge_ref, out_ref):
    misc = neighbour_sums(jnp.concatenate([got_ref[...], jnp.zeros((128, 128 - ROWS), f32)], axis=1), m_ref[...]) + edge_ref[...]
    for t in range(OWN):
        out_ref[pl.ds(t, 128, stride=FIRST), :] = sums_ref[t * 128 : (t + 1) * 128, 0:128]
        out_ref[pl.ds(OWN + t, 128, stride=FIRST), :] = sums_ref[t * 128 : (t + 1) * 128, 128:256]
    out_ref[pl.ds(2 * OWN, 128, stride=FIRST), :] = misc


def passed_on(misc):
    lane, row = iota((128, 128), 1), iota((128, 128), 0)
    gx, gy = row >> 3, row & 7
    out = jnp.where((lane >= 64) & (lane < 80) & (gx < 15), pltpu.roll(misc, 120, 0), 0.0)
    out = jnp.where((lane >= 80) & (lane < 96) & (gx > 0), pltpu.roll(misc, 8, 0), out)
    out = jnp.where((lane >= 96) & (lane < 100) & (gy < 7), pltpu.roll(misc, 127, 0), out)
    return jnp.where((lane >= 100) & (lane < 104) & (gy > 0), pltpu.roll(misc, 1, 0), out)


def advance(state_ref, misc, cchi, count_ref, cols, weight_ref, out_ref, last):
    count = count_ref[...]
    fraction = 1.0 / count
    mixing = fraction * mixing_rate * jnp.concatenate(
        [jnp.broadcast_to(cchi[t], (SPEC, ETA)) for t in range(OWN)], axis=0
    )
    reacting = fraction * react_rate
    near = misc.T[:ROWS]
    state = state_ref[...]
    state = state + coupling * (near - 6.0 * state)
    lane = iota((ROWS, ETA), 1)

    def substep(index, current):
        speed = jnp.tanh(current)
        source = []
        for t in range(OWN):
            parts = [speed[t * SPEC + s : t * SPEC + s + 1] * cols[s] for s in range(SPEC)]
            while len(parts) > 1:
                parts = [a + b for a, b in zip(parts[::2], parts[1::2])]
            source.append(parts[0])
        source = jnp.concatenate(source, axis=0)
        left = jnp.where(lane == 0, current, pltpu.roll(current, 1, 1))
        right = jnp.where(lane == ETA - 1, current, pltpu.roll(current, ETA - 1, 1))
        update = mixing * (right - 2.0 * current + left) + reacting * source
        return jnp.where(index.astype(f32) < count, current + update, current)

    state = lax.fori_loop(0, SUBMAX, substep, state)
    state_ref_out, pay = out_ref
    state_ref_out[...] = state
    weight = weight_ref[...]
    for t in range(OWN):
        theta = jnp.sum(weight * state[t * SPEC : (t + 1) * SPEC], axis=0, keepdims=True)
        pay[pl.ds(t, 128, stride=LATER), :] = jnp.broadcast_to(theta, (128, ETA))
    out = passed_on(misc)
    if not last:
        out = out + jnp.concatenate([state, jnp.zeros((128 - ROWS, ETA), f32)], axis=0).T
    pay[pl.ds(OWN, 128, stride=LATER), :] = out


def total_of(got_ref, row, stride):
    return jnp.sum(got_ref[pl.ds(row, 128, stride=stride), :], axis=0, keepdims=True)


def first_advance_kernel(
    got_ref, state_ref, count_ref, cols, weight_ref, state_out, weight_out, pay
):
    cchi = []
    for t in range(OWN):
        w = total_of(got_ref, t, FIRST)
        n = total_of(got_ref, OWN + t, FIRST)
        weight_out[t : t + 1, :] = w
        cchi.append((n + prior_flux) / (w + prior_weight))
    misc = got_ref[pl.ds(2 * OWN, 128, stride=FIRST), :]
    advance(state_ref, misc, cchi, count_ref, cols, weight_ref, (state_out, pay), False)


def later_advance_kernel(
    got_ref, state_ref, mass_ref, count_ref, cols, weight_ref, state_out, pay
):
    cchi = []
    for t in range(OWN):
        n = total_of(got_ref, t, LATER)
        cchi.append((n + prior_flux) / (mass_ref[t : t + 1, :] + prior_weight))
    misc = got_ref[pl.ds(OWN, 128, stride=LATER), :]
    advance(state_ref, misc, cchi, count_ref, cols, weight_ref, (state_out, pay), True)


def fine_update(got_ref, misc, t_ref, e_ref, rinv_ref, lab_ref, rs_ref, par_ref, tfine, grid):
    theta = jnp.concatenate([got_ref[pl.ds(t, 128, stride=LATER), :] for t in range(OWN)], axis=0)
    picked = dot(rs_ref[...], jnp.concatenate(halves(theta), axis=1), TN).astype(bf16)
    high, low = picked[:, :128], picked[:, 128:]
    rows = jnp.concatenate(
        [jnp.concatenate([high, high], axis=1), jnp.concatenate([low, low], axis=1)], axis=0
    )
    lab = lab_ref[...]

    def weigh(group, carry):
        means = dot(rows, e_ref[group], NN)
        means = means[:LABELS] + means[LABELS:]
        par_rows, inverse = rows_of(par_ref, group), rows_of(rinv_ref, group)
        out = []
        for q in range(8):
            mine = lab == par_rows[q : q + 1]
            out.append(jnp.sum(jnp.where(mine, means[:, q * 128 : (q + 1) * 128], 0.0), axis=0, keepdims=True))
        put_rows(tfine, group, [jnp.concatenate(out, axis=0) * inverse])
        return carry

    lax.fori_loop(0, GROUPS, weigh, 0, unroll=UNROLL)
    beside = misc.T
    t = t_ref[...]
    grid[1:5, 8:24, :] = t.reshape(4, 16, 128)
    grid[5, 8:24, :] = beside[64:80]
    grid[0, 8:24, :] = beside[80:96]
    for x in range(4):
        grid[1 + x, 24:25, :] = beside[96 + x : 97 + x]
        grid[1 + x, 7:8, :] = beside[100 + x : 101 + x]
    around = grid[2:6, 8:24, :] + grid[0:4, 8:24, :]
    around = around + grid[1:5, 9:25, :] + grid[1:5, 7:23, :]
    around = around.reshape(ROWS, 128)
    lane = iota((ROWS, 128), 1)
    around = around + jnp.where(lane == 127, 0.0, pltpu.roll(t, 127, 1))
    around = around + jnp.where(lane == 0, 0.0, pltpu.roll(t, 1, 1))
    return t + thermal_diffusion * (around - 6.0 * t) + damping_contribution * (tfine[...] - t)


def middle_kernel(
    got_ref, t_ref, e_ref, rinv_ref, mb_ref, lab_ref, rs_ref, m_ref, par_ref, who_ref,
    t_out, pay, tfine, grid, flux, arms, acc, edge,
):
    misc = got_ref[pl.ds(OWN, 128, stride=LATER), :]
    t = fine_update(got_ref, misc, t_ref, e_ref, rinv_ref, lab_ref, rs_ref, par_ref, tfine, grid)
    t_out[...] = t
    flux[...] = mb_ref[...] * (1.0 + 0.5 * jnp.tanh(t))
    acc[...] = jnp.zeros_like(acc)

    def gather(group, carry):
        flux_rows = rows_of(flux, group)
        for q in range(8):
            at = slice(q * 128, (q + 1) * 128)
            for k, part in enumerate(halves(flux_rows[q : q + 1])):
                arms[k * LABELS : (k + 1) * LABELS, at] = who_ref[group, :, at] * part
        acc[...] += dot(arms[...], e_ref[group, 0:128], NT)
        return carry

    lax.fori_loop(0, GROUPS, gather, 0, unroll=UNROLL)
    both = acc[...]
    sums = to_slots(rs_ref[...], both[0:48] + both[48:96])
    for k in range(OWN):
        pay[pl.ds(k, 128, stride=LATER), :] = sums[k * 128 : (k + 1) * 128]
    out = neighbour_sums(misc, m_ref[...]) + edges_by_z(t_out, edge)
    pay[pl.ds(OWN, 128, stride=LATER), :] = out


def final_kernel(got_ref, t_ref, e_ref, rinv_ref, lab_ref, rs_ref, par_ref, t_out, tfine, grid):
    misc = got_ref[pl.ds(OWN, 128, stride=LATER), :]
    t_out[...] = fine_update(got_ref, misc, t_ref, e_ref, rinv_ref, lab_ref, rs_ref, par_ref, tfine, grid)


def call(kernel, outs, scratch, *operands, scalars=0, results=(), streamed=()):
    vmem, smem = pl.BlockSpec(memory_space=pltpu.VMEM), pl.BlockSpec(memory_space=pltpu.SMEM)
    away = set(results) | set(streamed)
    return pl.pallas_call(
        kernel,
        out_shape=[pltpu.HBM(*o) if i in away else pltpu.VMEM(*o) for i, o in enumerate(outs)],
        in_specs=[smem] * scalars + [vmem] * (len(operands) - scalars),
        out_specs=[pl.BlockSpec(memory_space=pl.ANY) if i in streamed else vmem for i in range(len(outs))],
        scratch_shapes=[pltpu.VMEM(*s) if isinstance(s, tuple) else s for s in scratch],
        compiler_params=pltpu.CompilerParams(vmem_limit_bytes=24 << 20),
    )(*operands)


def exchange(array):
    rows = array.shape[0] // DEV
    sent = array.reshape(DEV, 1, rows * 128)
    return lax.all_to_all(sent, ("gx", "gy"), 0, 0, tiled=True).reshape(array.shape)


def from_hbm(*arrays):
    return [pltpu.with_memory_space_constraint(a, pltpu.HBM) for a in arrays]


def shards(thermal, average, variance, mass, bare, parent, species, position, partners, increments, chem, weight):
    dev = (lax.axis_index("gx") * 8 + lax.axis_index("gy")).astype(jnp.int32).reshape(1)
    fine = [a.reshape(ROWS, 128) for a in (thermal, average, variance, mass, bare, parent)]
    t0, av, var, mass, bare, par = fine
    state = species.reshape(ROWS, ETA)
    bp, ri, sw = position.reshape(1, SLOTS), increments.reshape(1, SLOTS), weight.reshape(1, SPEC)
    cells = ((ROWS, 128), f32)
    square = ((128, 128), f32)
    pay = ((DEV * LATER, 128), f32)

    states = lax.all_to_all(state.T.reshape(DEV, 1, ROWS), ("gx", "gy"), 0, 0, tiled=True).reshape(DEV, ROWS)
    table, mb, rinv, lab, rs, m, sums, edges, count, cols, sw, who = call(
        prep_kernel,
        [((GROUPS, 256, WIDE), bf16), cells, cells, ((LABELS, 128), jnp.int32), ((SLOTS, LABELS), bf16),
         ((SLOTS, SLOTS), bf16), ((SLOTS, 256), f32), square, cells, ((SPEC, SPEC, ETA), f32), ((SPEC, ETA), f32),
         ((GROUPS, LABELS, WIDE), bf16)],
        [square, square, cells, cells, cells, ((4 * LABELS, WIDE), bf16),
         ((4 * LABELS, 128), f32), ((GROUPS, 256, WIDE), bf16), square, pltpu.SemaphoreType.DMA((GROUPS,))],
        dev, *from_hbm(t0, av, var, mass, bare, par, bp, partners.T, ri, chem, sw), scalars=1, streamed=(0,),
    )
    (sent,) = call(first_pack_kernel, [((DEV * FIRST, 128), f32)], [], states, m, sums, edges)
    got = exchange(sent)
    state, own_weight, sent = call(
        first_advance_kernel, [((ROWS, ETA), f32), ((8, 128), f32), pay], [],
        got, *from_hbm(state), count, cols, sw,
    )
    got = exchange(sent)
    grid = ((6, 32, 128), f32)
    t1, sent = call(
        middle_kernel, [cells, pay],
        [cells, grid, cells, ((2 * LABELS, WIDE), bf16), ((2 * LABELS, 128), f32), square],
        got, t0, table, rinv, mb, lab, rs, m, par, who,
    )
    got = exchange(sent)
    state, sent = call(
        later_advance_kernel, [((ROWS, ETA), f32), pay], [],
        got, state, own_weight, count, cols, sw, results=(0,),
    )
    got = exchange(sent)
    (t2,) = call(final_kernel, [cells], [cells, grid], got, t1, table, rinv, lab, rs, par, results=(0,))
    return state.reshape(species.shape), t2.reshape(thermal.shape)


def solution(mesh):
    fine = P("gx", "gy", None)
    slots = P(("gx", "gy"), None, None)
    return jax.shard_map(
        shards,
        mesh=mesh,
        in_specs=(fine,) * 6 + (slots,) + (P(),) * 5,
        out_specs=(slots, fine),
        check_vma=False,
    )
```

```python
import jax
import jax.numpy as jnp
from jax import lax
from jax.experimental import pallas as pl
from jax.experimental.pallas import tpu as pltpu
from jax.sharding import PartitionSpec as P

DEV = 128
OWN = 4
SLOTS = 512
SPEC = 16
ETA = 128
ROWS = 64
SUBMAX = 16
LABELS = 48
GROUPS = 8
WIDE = 1024
FIRST = 9
LATER = 5
UNROLL = 8
SUBROLL = 4
LOG2E = 1.4426950408889634

coupling = 0.05
mixing_rate = 0.2
react_rate = 0.5
prior_weight = 1.0
prior_flux = 0.5
thermal_diffusion = 0.1
damping_contribution = 0.3

f32 = jnp.float32
bf16 = jnp.bfloat16
NN = ((1,), (0,))
NT = ((1,), (1,))
TN = ((0,), (0,))


def dot(a, b, dims):
    return lax.dot_general(a, b, (dims, ((), ())), preferred_element_type=f32)


def iota(shape, dim):
    return lax.broadcasted_iota(jnp.int32, shape, dim)


def halves(x):
    high = x.astype(bf16)
    return high, (x - high.astype(f32)).astype(bf16)


def hot(mask):
    return jnp.where(mask, 1.0, 0.0).astype(bf16)


def marked(mask):
    return jnp.where(mask, jnp.ones((), bf16), jnp.zeros((), bf16))


def together(ref, group, count):
    return jnp.concatenate([ref[group * 8 + q, 0:count, :] for q in range(8)], axis=1)


def rows_of(ref, group):
    return ref[pl.ds(pl.multiple_of(group * 8, 8), 8), :]


def put_rows(ref, group, rows):
    ref[pl.ds(pl.multiple_of(group * 8, 8), 8), :] = jnp.concatenate(rows, axis=0)


def to_slots(rs, sums):
    both = dot(rs, jnp.concatenate(halves(sums), axis=1), NN)
    return both[:, : sums.shape[1]] + both[:, sums.shape[1] :]


def prep_kernel(
    dev_ref, t_ref, av_ref, var_ref, mass_ref, bare_ref, par_ref, bp_ref, fp_ref, ri_ref, c_ref, sw_ref,
    e_out, mb_ref, rinv_ref, lab_ref, rs_ref, m_ref, sums_ref, edge_ref, count_ref, cols, weight_ref, who_ref,
    le, l1e, a1, b1, chi, acc, e_ref, edge, sems,
):
    edge_ref[...] = edges_by_z(t_ref, edge)
    for s in range(SPEC):
        cols[s] = jnp.broadcast_to(c_ref[:, s : s + 1], (SPEC, ETA))
    weight_ref[...] = jnp.broadcast_to(
        jnp.sum(
            jnp.where(iota((SPEC, SPEC), 0) == iota((SPEC, SPEC), 1), sw_ref[...], 0.0), axis=1, keepdims=True
        ),
        (SPEC, ETA),
    )
    own = bp_ref[...] == dev_ref[0] * OWN + (iota((ROWS, SLOTS), 0) >> 4)
    count = jnp.sum(jnp.where(own, ri_ref[...] + 1, 0).astype(f32), axis=1, keepdims=True)
    count_ref[...] = jnp.broadcast_to(count, (ROWS, ETA))

    named = jnp.zeros((32, 16), f32)
    for group in range(GROUPS):
        rows = par_ref[group * 8 : (group + 1) * 8, :]
        tall, short = rows >> 4, rows & 15
        tall = jnp.concatenate([hot(tall[q : q + 1] == iota((32, 128), 0)) for q in range(8)], axis=1)
        short = jnp.concatenate([hot(short[q : q + 1] == iota((16, 128), 0)) for q in range(8)], axis=1)
        named = named + dot(tall, short, NT)
    named = hot(named > 0.5)
    within = dot(named, hot(iota((16, 16), 0) < iota((16, 16), 1)), NN)
    ahead = dot(hot(iota((32, 32), 1) < iota((32, 32), 0)), named, NN).astype(bf16)
    ahead = dot(ahead, jnp.ones((16, 16), bf16), NN)
    order = jnp.where(named > 0, within + ahead + 1.0, 0.0).astype(bf16)
    spread = dot(hot(iota((SLOTS, 32), 0) >> 4 == iota((SLOTS, 32), 1)), order, NN)
    spread = jnp.where(iota((SLOTS, 16), 0) & 15 == iota((SLOTS, 16), 1), spread, 0.0).astype(bf16)
    order = dot(spread, jnp.ones((16, 128), bf16), NN)
    sel = hot(order == (iota((SLOTS, 128), 1) + 1).astype(f32))
    cell = iota((SLOTS, 128), 0) + 1
    label = dot(
        sel,
        jnp.concatenate([(cell >> 4).astype(f32).astype(bf16), (cell & 15).astype(f32).astype(bf16)], axis=1),
        TN,
    )
    lab = ((label[:, :128] * 16.0 + label[:, 128:]).astype(jnp.int32) - 1)[:LABELS]
    lab_ref[...] = lab

    bp = bp_ref[...]
    device = iota((128, SLOTS), 0).astype(f32).astype(bf16)
    pt = jnp.concatenate(
        [
            marked(jnp.where(bp & 3 == t, bp >> 2, -1).astype(f32).astype(bf16) == device)
            for t in range(OWN)
        ],
        axis=0,
    )
    rs = dot(pt, sel, NN).astype(bf16)[:, :LABELS]
    rs_ref[...] = rs
    other = iota((256, SLOTS), 0).astype(f32).astype(bf16)
    near = fp_ref[...]
    adjacent = []
    for half in range(2):
        part = near - 256 * half
        part = jnp.where((part >= 0) & (part < 256), part, -1).astype(f32)
        total = jnp.zeros((256, SLOTS), bf16)
        for j in range(6):
            total = total + marked(part[j : j + 1].astype(bf16) == other)
        adjacent.append(total)
    half = dot(pt, jnp.concatenate(adjacent, axis=0), NT).astype(bf16)
    m_ref[...] = dot(half, pt, NT).astype(bf16)

    point = (iota((ETA, 128), 0).astype(f32) + 0.5) / ETA
    le[...] = jnp.log(point) * LOG2E
    l1e[...] = jnp.log(1.0 - point) * LOG2E
    shape_sum = 1.0 / var_ref[...] - 1.0
    a1[...] = av_ref[...] * shape_sum - 1.0
    b1[...] = (1.0 - av_ref[...]) * shape_sum - 1.0
    chi[...] = bare_ref[...] * (1.0 + 0.5 * jnp.tanh(t_ref[...]))
    acc[...] = jnp.zeros_like(acc)

    def tables(group, carry):
        a_rows, b_rows = rows_of(a1, group), rows_of(b1, group)
        chi_rows, mass_rows, par_rows = rows_of(chi, group), rows_of(mass_ref, group), rows_of(par_ref, group)
        inverse, mass_over, arms = [], [], []
        for q in range(8):
            logits = a_rows[q : q + 1] * le[...] + b_rows[q : q + 1] * l1e[...]
            table = jnp.exp2(logits - jnp.max(logits, axis=0, keepdims=True))
            r = 1.0 / jnp.sum(table, axis=0, keepdims=True)
            high, low = halves(table)
            e_ref[group * 8 + q, 0:128, :] = high
            e_ref[group * 8 + q, 128:256, :] = low
            w = mass_rows[q : q + 1] * r
            n = w * chi_rows[q : q + 1]
            inverse.append(r)
            mass_over.append(w)
            mine = hot(lab == par_rows[q : q + 1])
            who_ref[group * 8 + q] = mine
            arms.append(jnp.concatenate([mine * part for part in (*halves(w), *halves(n))], axis=0))
        put_rows(rinv_ref, group, inverse)
        put_rows(mb_ref, group, [jnp.concatenate(mass_over, axis=0) * rows_of(bare_ref, group)])
        pltpu.make_async_copy(e_ref.at[pl.ds(group * 8, 8)], e_out.at[pl.ds(group * 8, 8)], sems.at[group]).start()
        acc[...] += dot(jnp.concatenate(arms, axis=1), together(e_ref, group, 128), NT)
        return carry

    lax.fori_loop(0, GROUPS, tables, 0, unroll=UNROLL)
    both = acc[...]
    w48 = both[0:48] + both[48:96]
    n48 = both[96:144] + both[144:192]
    sums_ref[...] = to_slots(rs, jnp.concatenate([w48, n48], axis=1))
    for group in range(GROUPS):
        pltpu.make_async_copy(e_ref.at[pl.ds(group * 8, 8)], e_out.at[pl.ds(group * 8, 8)], sems.at[group]).wait()


def neighbour_sums(part, m):
    lane = iota((128, 128), 1)
    stacked = jnp.concatenate([jnp.where(lane >> 4 == t, part, 0.0) for t in range(OWN)], axis=0)
    high, low = halves(stacked)
    both = dot(m, jnp.concatenate([high, low], axis=1), NN)
    total = both[:, :128] + both[:, 128:]
    for shift in (64, 32, 16):
        total = total + pltpu.roll(total, shift, 1)
    out = jnp.zeros((128, 128), f32)
    for t in range(OWN):
        out = jnp.where(lane >> 4 == t, total[t * 128 : (t + 1) * 128], out)
    return out


def edges_by_z(t_ref, edge):
    edge[...] = jnp.zeros_like(edge)
    edge[64:80, :] = t_ref[0:16, :]
    edge[80:96, :] = t_ref[48:64, :]
    for x in range(4):
        edge[96 + x : 97 + x, :] = t_ref[16 * x : 16 * x + 1, :]
        edge[100 + x : 101 + x, :] = t_ref[16 * x + 15 : 16 * x + 16, :]
    return edge[...].T


def first_pack_kernel(got_ref, m_ref, sums_ref, edge_ref, out_ref):
    misc = neighbour_sums(jnp.concatenate([got_ref[...], jnp.zeros((128, 128 - ROWS), f32)], axis=1), m_ref[...]) + edge_ref[...]
    for t in range(OWN):
        out_ref[pl.ds(t, 128, stride=FIRST), :] = sums_ref[t * 128 : (t + 1) * 128, 0:128]
        out_ref[pl.ds(OWN + t, 128, stride=FIRST), :] = sums_ref[t * 128 : (t + 1) * 128, 128:256]
    out_ref[pl.ds(2 * OWN, 128, stride=FIRST), :] = misc


def passed_on(misc):
    lane, row = iota((128, 128), 1), iota((128, 128), 0)
    gx, gy = row >> 3, row & 7
    out = jnp.where((lane >= 64) & (lane < 80) & (gx < 15), pltpu.roll(misc, 120, 0), 0.0)
    out = jnp.where((lane >= 80) & (lane < 96) & (gx > 0), pltpu.roll(misc, 8, 0), out)
    out = jnp.where((lane >= 96) & (lane < 100) & (gy < 7), pltpu.roll(misc, 127, 0), out)
    return jnp.where((lane >= 100) & (lane < 104) & (gy > 0), pltpu.roll(misc, 1, 0), out)


def advance(state_ref, misc, cchi, count_ref, cols, weight_ref, speed_ref, out_ref, last):
    count = count_ref[...]
    fraction = 1.0 / count
    mixing = fraction * mixing_rate * jnp.concatenate(
        [jnp.broadcast_to(cchi[t], (SPEC, ETA)) for t in range(OWN)], axis=0
    )
    reacting = fraction * react_rate
    near = misc.T[:ROWS]
    state = state_ref[...]
    state = state + coupling * (near - 6.0 * state)
    lane = iota((8, ETA), 1)
    pieces = [slice(p * 8, (p + 1) * 8) for p in range(8)]

    def substep(index, states):
        for p, current in enumerate(states):
            speed_ref[pieces[p]] = jnp.tanh(current)
        out = list(states)
        for t in range(OWN):
            speed = [speed_ref[pl.ds(t * SPEC + s, 8, stride=0), :] for s in range(SPEC)]
            for half in range(2):
                p = 2 * t + half
                current = states[p]
                parts = [speed[s] * cols[s, half * 8 : half * 8 + 8] for s in range(SPEC)]
                while len(parts) > 1:
                    parts = [a + b for a, b in zip(parts[::2], parts[1::2])]
                left = jnp.where(lane == 0, current, pltpu.roll(current, 1, 1))
                right = jnp.where(lane == ETA - 1, current, pltpu.roll(current, ETA - 1, 1))
                update = mixing[pieces[p]] * (right - 2.0 * current + left) + reacting[pieces[p]] * parts[0]
                out[p] = jnp.where(index.astype(f32) < count[pieces[p]], current + update, current)
        return tuple(out)

    state = jnp.concatenate(
        lax.fori_loop(0, SUBMAX, substep, tuple(state[p] for p in pieces), unroll=SUBROLL), axis=0
    )
    state_ref_out, pay = out_ref
    state_ref_out[...] = state
    weight = weight_ref[...]
    for t in range(OWN):
        theta = jnp.sum(weight * state[t * SPEC : (t + 1) * SPEC], axis=0, keepdims=True)
        pay[pl.ds(t, 128, stride=LATER), :] = jnp.broadcast_to(theta, (128, ETA))
    out = passed_on(misc)
    if not last:
        out = out + jnp.concatenate([state, jnp.zeros((128 - ROWS, ETA), f32)], axis=0).T
    pay[pl.ds(OWN, 128, stride=LATER), :] = out


def total_of(got_ref, row, stride):
    return jnp.sum(got_ref[pl.ds(row, 128, stride=stride), :], axis=0, keepdims=True)


def first_advance_kernel(
    got_ref, state_ref, count_ref, cols, weight_ref, state_out, weight_out, pay, speed_ref
):
    cchi = []
    for t in range(OWN):
        w = total_of(got_ref, t, FIRST)
        n = total_of(got_ref, OWN + t, FIRST)
        weight_out[t : t + 1, :] = w
        cchi.append((n + prior_flux) / (w + prior_weight))
    misc = got_ref[pl.ds(2 * OWN, 128, stride=FIRST), :]
    advance(state_ref, misc, cchi, count_ref, cols, weight_ref, speed_ref, (state_out, pay), False)


def later_advance_kernel(
    got_ref, state_ref, mass_ref, count_ref, cols, weight_ref, state_out, pay, speed_ref
):
    cchi = []
    for t in range(OWN):
        n = total_of(got_ref, t, LATER)
        cchi.append((n + prior_flux) / (mass_ref[t : t + 1, :] + prior_weight))
    misc = got_ref[pl.ds(OWN, 128, stride=LATER), :]
    advance(state_ref, misc, cchi, count_ref, cols, weight_ref, speed_ref, (state_out, pay), True)


def fine_update(got_ref, misc, t_ref, e_ref, rinv_ref, lab_ref, rs_ref, par_ref, tfine, grid):
    theta = jnp.concatenate([got_ref[pl.ds(t, 128, stride=LATER), :] for t in range(OWN)], axis=0)
    picked = dot(rs_ref[...], jnp.concatenate(halves(theta), axis=1), TN).astype(bf16)
    high, low = picked[:, :128], picked[:, 128:]
    rows = jnp.concatenate(
        [jnp.concatenate([high, high], axis=1), jnp.concatenate([low, low], axis=1)], axis=0
    )
    lab = lab_ref[...]

    def weigh(group, carry):
        means = dot(rows, together(e_ref, group, 256), NN)
        means = means[:LABELS] + means[LABELS:]
        par_rows, inverse = rows_of(par_ref, group), rows_of(rinv_ref, group)
        out = []
        for q in range(8):
            mine = lab == par_rows[q : q + 1]
            out.append(jnp.sum(jnp.where(mine, means[:, q * 128 : (q + 1) * 128], 0.0), axis=0, keepdims=True))
        put_rows(tfine, group, [jnp.concatenate(out, axis=0) * inverse])
        return carry

    lax.fori_loop(0, GROUPS, weigh, 0, unroll=UNROLL)
    beside = misc.T
    t = t_ref[...]
    grid[1:5, 8:24, :] = t.reshape(4, 16, 128)
    grid[5, 8:24, :] = beside[64:80]
    grid[0, 8:24, :] = beside[80:96]
    for x in range(4):
        grid[1 + x, 24:25, :] = beside[96 + x : 97 + x]
        grid[1 + x, 7:8, :] = beside[100 + x : 101 + x]
    around = grid[2:6, 8:24, :] + grid[0:4, 8:24, :]
    around = around + grid[1:5, 9:25, :] + grid[1:5, 7:23, :]
    around = around.reshape(ROWS, 128)
    lane = iota((ROWS, 128), 1)
    around = around + jnp.where(lane == 127, 0.0, pltpu.roll(t, 127, 1))
    around = around + jnp.where(lane == 0, 0.0, pltpu.roll(t, 1, 1))
    return t + thermal_diffusion * (around - 6.0 * t) + damping_contribution * (tfine[...] - t)


def middle_kernel(
    got_ref, t_ref, e_ref, rinv_ref, mb_ref, lab_ref, rs_ref, m_ref, par_ref, who_ref,
    t_out, pay, tfine, grid, flux, acc, edge,
):
    misc = got_ref[pl.ds(OWN, 128, stride=LATER), :]
    t = fine_update(got_ref, misc, t_ref, e_ref, rinv_ref, lab_ref, rs_ref, par_ref, tfine, grid)
    t_out[...] = t
    flux[...] = mb_ref[...] * (1.0 + 0.5 * jnp.tanh(t))
    acc[...] = jnp.zeros_like(acc)

    def gather(group, carry):
        flux_rows = rows_of(flux, group)
        arms = []
        for q in range(8):
            mine = who_ref[group * 8 + q]
            arms.append(jnp.concatenate([mine * part for part in halves(flux_rows[q : q + 1])], axis=0))
        acc[...] += dot(jnp.concatenate(arms, axis=1), together(e_ref, group, 128), NT)
        return carry

    lax.fori_loop(0, GROUPS, gather, 0, unroll=UNROLL)
    both = acc[...]
    sums = to_slots(rs_ref[...], both[0:48] + both[48:96])
    for k in range(OWN):
        pay[pl.ds(k, 128, stride=LATER), :] = sums[k * 128 : (k + 1) * 128]
    out = neighbour_sums(misc, m_ref[...]) + edges_by_z(t_out, edge)
    pay[pl.ds(OWN, 128, stride=LATER), :] = out


def final_kernel(got_ref, t_ref, e_ref, rinv_ref, lab_ref, rs_ref, par_ref, t_out, tfine, grid):
    misc = got_ref[pl.ds(OWN, 128, stride=LATER), :]
    t_out[...] = fine_update(got_ref, misc, t_ref, e_ref, rinv_ref, lab_ref, rs_ref, par_ref, tfine, grid)


def call(kernel, outs, scratch, *operands, scalars=0, results=(), streamed=()):
    vmem, smem = pl.BlockSpec(memory_space=pltpu.VMEM), pl.BlockSpec(memory_space=pltpu.SMEM)
    away = set(results) | set(streamed)
    return pl.pallas_call(
        kernel,
        out_shape=[pltpu.HBM(*o) if i in away else pltpu.VMEM(*o) for i, o in enumerate(outs)],
        in_specs=[smem] * scalars + [vmem] * (len(operands) - scalars),
        out_specs=[pl.BlockSpec(memory_space=pl.ANY) if i in streamed else vmem for i in range(len(outs))],
        scratch_shapes=[pltpu.VMEM(*s) if isinstance(s, tuple) else s for s in scratch],
        compiler_params=pltpu.CompilerParams(vmem_limit_bytes=24 << 20),
    )(*operands)


def exchange(array):
    rows = array.shape[0] // DEV
    sent = array.reshape(DEV, 1, rows * 128)
    return lax.all_to_all(sent, ("gx", "gy"), 0, 0, tiled=True).reshape(array.shape)


def from_hbm(*arrays):
    return [pltpu.with_memory_space_constraint(a, pltpu.HBM) for a in arrays]


def shards(thermal, average, variance, mass, bare, parent, species, position, partners, increments, chem, weight):
    dev = (lax.axis_index("gx") * 8 + lax.axis_index("gy")).astype(jnp.int32).reshape(1)
    fine = [a.reshape(ROWS, 128) for a in (thermal, average, variance, mass, bare, parent)]
    t0, av, var, mass, bare, par = fine
    state = species.reshape(ROWS, ETA)
    bp, ri, sw = position.reshape(1, SLOTS), increments.reshape(1, SLOTS), weight.reshape(1, SPEC)
    cells = ((ROWS, 128), f32)
    square = ((128, 128), f32)
    pay = ((DEV * LATER, 128), f32)

    states = lax.all_to_all(state.T.reshape(DEV, 1, ROWS), ("gx", "gy"), 0, 0, tiled=True).reshape(DEV, ROWS)
    table, mb, rinv, lab, rs, m, sums, edges, count, cols, sw, who = call(
        prep_kernel,
        [((ROWS, 256, 128), bf16), cells, cells, ((LABELS, 128), jnp.int32), ((SLOTS, LABELS), bf16),
         ((SLOTS, SLOTS), bf16), ((SLOTS, 256), f32), square, cells, ((SPEC, SPEC, ETA), f32), ((SPEC, ETA), f32),
         ((ROWS, LABELS, 128), bf16)],
        [square, square, cells, cells, cells, ((4 * LABELS, 128), f32), ((ROWS, 256, 128), bf16), square, pltpu.SemaphoreType.DMA((GROUPS,))],
        dev, *from_hbm(t0, av, var, mass, bare, par, bp, partners.T, ri, chem, sw), scalars=1, streamed=(0,),
    )
    (sent,) = call(first_pack_kernel, [((DEV * FIRST, 128), f32)], [], states, m, sums, edges)
    got = exchange(sent)
    state, own_weight, sent = call(
        first_advance_kernel, [((ROWS, ETA), f32), ((8, 128), f32), pay], [cells],
        got, *from_hbm(state), count, cols, sw,
    )
    got = exchange(sent)
    grid = ((6, 32, 128), f32)
    t1, sent = call(
        middle_kernel, [cells, pay],
        [cells, grid, cells, ((2 * LABELS, 128), f32), square],
        got, t0, table, rinv, mb, lab, rs, m, par, who,
    )
    got = exchange(sent)
    state, sent = call(
        later_advance_kernel, [((ROWS, ETA), f32), pay], [cells],
        got, state, own_weight, count, cols, sw, results=(0,),
    )
    got = exchange(sent)
    (t2,) = call(final_kernel, [cells], [cells, grid], got, t1, table, rinv, lab, rs, par, results=(0,))
    return state.reshape(species.shape), t2.reshape(thermal.shape)


def solution(mesh):
    fine = P("gx", "gy", None)
    slots = P(("gx", "gy"), None, None)
    return jax.shard_map(
        shards,
        mesh=mesh,
        in_specs=(fine,) * 6 + (slots,) + (P(),) * 5,
        out_specs=(slots, fine),
        check_vma=False,
    )
```

```python
import jax
import jax.numpy as jnp
from jax import lax
from jax.experimental import pallas as pl
from jax.experimental.pallas import tpu as pltpu
from jax.sharding import PartitionSpec as P

DEV = 128
OWN = 4
SLOTS = 512
SPEC = 16
ETA = 128
ROWS = 64
SUBMAX = 16
LABELS = 48
GROUPS = 8
WIDE = 1024
FIRST = 9
LATER = 5
UNROLL = 8
SUBROLL = 4
LOG2E = 1.4426950408889634

coupling = 0.05
mixing_rate = 0.2
react_rate = 0.5
prior_weight = 1.0
prior_flux = 0.5
thermal_diffusion = 0.1
damping_contribution = 0.3

f32 = jnp.float32
bf16 = jnp.bfloat16
NN = ((1,), (0,))
NT = ((1,), (1,))
TN = ((0,), (0,))


def dot(a, b, dims):
    return lax.dot_general(a, b, (dims, ((), ())), preferred_element_type=f32)


def iota(shape, dim):
    return lax.broadcasted_iota(jnp.int32, shape, dim)


def halves(x):
    high = x.astype(bf16)
    return high, (x - high.astype(f32)).astype(bf16)


def hot(mask):
    return jnp.where(mask, 1.0, 0.0).astype(bf16)


def marked(mask):
    return jnp.where(mask, jnp.ones((), bf16), jnp.zeros((), bf16))


def together(ref, group, count):
    return jnp.concatenate([ref[group * 8 + q, 0:count, :] for q in range(8)], axis=1)


def rows_of(ref, group):
    return ref[pl.ds(pl.multiple_of(group * 8, 8), 8), :]


def put_rows(ref, group, rows):
    ref[pl.ds(pl.multiple_of(group * 8, 8), 8), :] = jnp.concatenate(rows, axis=0)


def to_slots(rs, sums):
    both = dot(rs, jnp.concatenate(halves(sums), axis=1), NN)
    return both[:, : sums.shape[1]] + both[:, sums.shape[1] :]


def prep_kernel(
    dev_ref, t_ref, av_ref, var_ref, mass_ref, bare_ref, par_ref, bp_ref, fp_ref, ri_ref, c_ref, sw_ref,
    e_out, mb_ref, rinv_ref, lab_ref, rs_ref, m_ref, sums_ref, edge_ref, count_ref, cols, weight_ref, who_ref,
    le, l1e, a1, b1, chi, acc, e_ref, edge, sems,
):
    edge_ref[...] = edges_by_z(t_ref, edge)
    for s in range(SPEC):
        cols[s] = jnp.broadcast_to(c_ref[:, s : s + 1], (SPEC, ETA))
    weight_ref[...] = jnp.broadcast_to(
        jnp.sum(
            jnp.where(iota((SPEC, SPEC), 0) == iota((SPEC, SPEC), 1), sw_ref[...], 0.0), axis=1, keepdims=True
        ),
        (SPEC, ETA),
    )
    own = bp_ref[...] == dev_ref[0] * OWN + (iota((ROWS, SLOTS), 0) >> 4)
    count = jnp.sum(jnp.where(own, ri_ref[...] + 1, 0).astype(f32), axis=1, keepdims=True)
    count_ref[...] = jnp.broadcast_to(count, (ROWS, ETA))

    named = jnp.zeros((32, 16), f32)
    for group in range(GROUPS):
        rows = par_ref[group * 8 : (group + 1) * 8, :]
        tall, short = rows >> 4, rows & 15
        tall = jnp.concatenate([hot(tall[q : q + 1] == iota((32, 128), 0)) for q in range(8)], axis=1)
        short = jnp.concatenate([hot(short[q : q + 1] == iota((16, 128), 0)) for q in range(8)], axis=1)
        named = named + dot(tall, short, NT)
    named = hot(named > 0.5)
    within = dot(named, hot(iota((16, 16), 0) < iota((16, 16), 1)), NN)
    ahead = dot(hot(iota((32, 32), 1) < iota((32, 32), 0)), named, NN).astype(bf16)
    ahead = dot(ahead, jnp.ones((16, 16), bf16), NN)
    order = jnp.where(named > 0, within + ahead + 1.0, 0.0).astype(bf16)
    spread = dot(hot(iota((SLOTS, 32), 0) >> 4 == iota((SLOTS, 32), 1)), order, NN)
    spread = jnp.where(iota((SLOTS, 16), 0) & 15 == iota((SLOTS, 16), 1), spread, 0.0).astype(bf16)
    order = dot(spread, jnp.ones((16, 128), bf16), NN)
    sel = hot(order == (iota((SLOTS, 128), 1) + 1).astype(f32))
    cell = iota((SLOTS, 128), 0) + 1
    label = dot(
        sel,
        jnp.concatenate([(cell >> 4).astype(f32).astype(bf16), (cell & 15).astype(f32).astype(bf16)], axis=1),
        TN,
    )
    lab = ((label[:, :128] * 16.0 + label[:, 128:]).astype(jnp.int32) - 1)[:LABELS]
    lab_ref[...] = lab

    bp = bp_ref[...]
    device = iota((128, SLOTS), 0).astype(f32).astype(bf16)
    pt = jnp.concatenate(
        [
            marked(jnp.where(bp & 3 == t, bp >> 2, -1).astype(f32).astype(bf16) == device)
            for t in range(OWN)
        ],
        axis=0,
    )
    rs = dot(pt, sel, NN).astype(bf16)[:, :LABELS]
    rs_ref[...] = rs
    other = iota((256, SLOTS), 0).astype(f32).astype(bf16)
    near = fp_ref[...]
    adjacent = []
    for half in range(2):
        part = near - 256 * half
        part = jnp.where((part >= 0) & (part < 256), part, -1).astype(f32)
        total = jnp.zeros((256, SLOTS), bf16)
        for j in range(6):
            total = total + marked(part[j : j + 1].astype(bf16) == other)
        adjacent.append(total)
    half = dot(pt, jnp.concatenate(adjacent, axis=0), NT).astype(bf16)
    m_ref[...] = dot(half, pt, NT).astype(bf16)

    point = (iota((ETA, 128), 0).astype(f32) + 0.5) / ETA
    le[...] = jnp.log(point) * LOG2E
    l1e[...] = jnp.log(1.0 - point) * LOG2E
    shape_sum = 1.0 / var_ref[...] - 1.0
    a1[...] = av_ref[...] * shape_sum - 1.0
    b1[...] = (1.0 - av_ref[...]) * shape_sum - 1.0
    chi[...] = bare_ref[...] * (1.0 + 0.5 * jnp.tanh(t_ref[...]))
    acc[...] = jnp.zeros_like(acc)

    def tables(group, carry):
        a_rows, b_rows = rows_of(a1, group), rows_of(b1, group)
        chi_rows, mass_rows, par_rows = rows_of(chi, group), rows_of(mass_ref, group), rows_of(par_ref, group)
        inverse, mass_over, arms = [], [], []
        for q in range(8):
            logits = a_rows[q : q + 1] * le[...] + b_rows[q : q + 1] * l1e[...]
            table = jnp.exp2(logits - jnp.max(logits, axis=0, keepdims=True))
            r = 1.0 / jnp.sum(table, axis=0, keepdims=True)
            high, low = halves(table)
            e_ref[group * 8 + q, 0:128, :] = high
            e_ref[group * 8 + q, 128:256, :] = low
            w = mass_rows[q : q + 1] * r
            n = w * chi_rows[q : q + 1]
            inverse.append(r)
            mass_over.append(w)
            mine = hot(lab == par_rows[q : q + 1])
            who_ref[group * 8 + q] = mine
            arms.append(jnp.concatenate([mine * part for part in (*halves(w), *halves(n))], axis=0))
        put_rows(rinv_ref, group, inverse)
        put_rows(mb_ref, group, [jnp.concatenate(mass_over, axis=0) * rows_of(bare_ref, group)])
        pltpu.make_async_copy(e_ref.at[pl.ds(group * 8, 8)], e_out.at[pl.ds(group * 8, 8)], sems.at[group]).start()
        acc[...] += dot(jnp.concatenate(arms, axis=1), together(e_ref, group, 128), NT)
        return carry

    lax.fori_loop(0, GROUPS, tables, 0, unroll=UNROLL)
    both = acc[...]
    w48 = both[0:48] + both[48:96]
    n48 = both[96:144] + both[144:192]
    sums_ref[...] = to_slots(rs, jnp.concatenate([w48, n48], axis=1))
    for group in range(GROUPS):
        pltpu.make_async_copy(e_ref.at[pl.ds(group * 8, 8)], e_out.at[pl.ds(group * 8, 8)], sems.at[group]).wait()


def neighbour_sums(part, m):
    lane = iota((128, 128), 1)
    stacked = jnp.concatenate([jnp.where(lane >> 4 == t, part, 0.0) for t in range(OWN)], axis=0)
    high, low = halves(stacked)
    both = dot(m, jnp.concatenate([high, low], axis=1), NN)
    total = both[:, :128] + both[:, 128:]
    for shift in (64, 32, 16):
        total = total + pltpu.roll(total, shift, 1)
    out = jnp.zeros((128, 128), f32)
    for t in range(OWN):
        out = jnp.where(lane >> 4 == t, total[t * 128 : (t + 1) * 128], out)
    return out


def edges_by_z(t_ref, edge):
    edge[...] = jnp.zeros_like(edge)
    edge[64:80, :] = t_ref[0:16, :]
    edge[80:96, :] = t_ref[48:64, :]
    for x in range(4):
        edge[96 + x : 97 + x, :] = t_ref[16 * x : 16 * x + 1, :]
        edge[100 + x : 101 + x, :] = t_ref[16 * x + 15 : 16 * x + 16, :]
    return edge[...].T


def load_kernel(*refs):
    half = (len(refs) - 1) // 2
    for source, target in zip(refs[:half], refs[half:]):
        target[...] = source[...]
    state = refs[0][...]
    refs[-1][...] = jnp.concatenate([state, state], axis=0).T[:, :ROWS]


def first_pack_kernel(got_ref, m_ref, sums_ref, edge_ref, out_ref):
    misc = neighbour_sums(jnp.concatenate([got_ref[...], jnp.zeros((128, 128 - ROWS), f32)], axis=1), m_ref[...]) + edge_ref[...]
    for t in range(OWN):
        out_ref[pl.ds(t, 128, stride=FIRST), :] = sums_ref[t * 128 : (t + 1) * 128, 0:128]
        out_ref[pl.ds(OWN + t, 128, stride=FIRST), :] = sums_ref[t * 128 : (t + 1) * 128, 128:256]
    out_ref[pl.ds(2 * OWN, 128, stride=FIRST), :] = misc


def passed_on(misc):
    lane, row = iota((128, 128), 1), iota((128, 128), 0)
    gx, gy = row >> 3, row & 7
    out = jnp.where((lane >= 64) & (lane < 80) & (gx < 15), pltpu.roll(misc, 120, 0), 0.0)
    out = jnp.where((lane >= 80) & (lane < 96) & (gx > 0), pltpu.roll(misc, 8, 0), out)
    out = jnp.where((lane >= 96) & (lane < 100) & (gy < 7), pltpu.roll(misc, 127, 0), out)
    return jnp.where((lane >= 100) & (lane < 104) & (gy > 0), pltpu.roll(misc, 1, 0), out)


def advance(state_ref, misc, cchi, count_ref, cols, weight_ref, speed_ref, out_ref, last):
    count = count_ref[...]
    fraction = 1.0 / count
    mixing = fraction * mixing_rate * jnp.concatenate(
        [jnp.broadcast_to(cchi[t], (SPEC, ETA)) for t in range(OWN)], axis=0
    )
    reacting = fraction * react_rate
    near = misc.T[:ROWS]
    state = state_ref[...]
    state = state + coupling * (near - 6.0 * state)
    lane = iota((8, ETA), 1)
    pieces = [slice(p * 8, (p + 1) * 8) for p in range(8)]

    def substep(index, states):
        for p, current in enumerate(states):
            speed_ref[pieces[p]] = jnp.tanh(current)
        out = list(states)
        for t in range(OWN):
            speed = [speed_ref[pl.ds(t * SPEC + s, 8, stride=0), :] for s in range(SPEC)]
            for half in range(2):
                p = 2 * t + half
                current = states[p]
                parts = [speed[s] * cols[s, half * 8 : half * 8 + 8] for s in range(SPEC)]
                while len(parts) > 1:
                    parts = [a + b for a, b in zip(parts[::2], parts[1::2])]
                left = jnp.where(lane == 0, current, pltpu.roll(current, 1, 1))
                right = jnp.where(lane == ETA - 1, current, pltpu.roll(current, ETA - 1, 1))
                update = mixing[pieces[p]] * (right - 2.0 * current + left) + reacting[pieces[p]] * parts[0]
                out[p] = jnp.where(index.astype(f32) < count[pieces[p]], current + update, current)
        return tuple(out)

    state = jnp.concatenate(
        lax.fori_loop(0, SUBMAX, substep, tuple(state[p] for p in pieces), unroll=SUBROLL), axis=0
    )
    state_ref_out, pay = out_ref
    state_ref_out[...] = state
    weight = weight_ref[...]
    for t in range(OWN):
        theta = jnp.sum(weight * state[t * SPEC : (t + 1) * SPEC], axis=0, keepdims=True)
        pay[pl.ds(t, 128, stride=LATER), :] = jnp.broadcast_to(theta, (128, ETA))
    out = passed_on(misc)
    if not last:
        out = out + jnp.concatenate([state, jnp.zeros((128 - ROWS, ETA), f32)], axis=0).T
    pay[pl.ds(OWN, 128, stride=LATER), :] = out


def total_of(got_ref, row, stride):
    return jnp.sum(got_ref[pl.ds(row, 128, stride=stride), :], axis=0, keepdims=True)


def first_advance_kernel(
    got_ref, state_ref, count_ref, cols, weight_ref, state_out, weight_out, pay, speed_ref
):
    cchi = []
    for t in range(OWN):
        w = total_of(got_ref, t, FIRST)
        n = total_of(got_ref, OWN + t, FIRST)
        weight_out[t : t + 1, :] = w
        cchi.append((n + prior_flux) / (w + prior_weight))
    misc = got_ref[pl.ds(2 * OWN, 128, stride=FIRST), :]
    advance(state_ref, misc, cchi, count_ref, cols, weight_ref, speed_ref, (state_out, pay), False)


def later_advance_kernel(
    got_ref, state_ref, mass_ref, count_ref, cols, weight_ref, state_out, pay, speed_ref
):
    cchi = []
    for t in range(OWN):
        n = total_of(got_ref, t, LATER)
        cchi.append((n + prior_flux) / (mass_ref[t : t + 1, :] + prior_weight))
    misc = got_ref[pl.ds(OWN, 128, stride=LATER), :]
    advance(state_ref, misc, cchi, count_ref, cols, weight_ref, speed_ref, (state_out, pay), True)


def fine_update(got_ref, misc, t_ref, e_ref, rinv_ref, lab_ref, rs_ref, par_ref, tfine, grid):
    theta = jnp.concatenate([got_ref[pl.ds(t, 128, stride=LATER), :] for t in range(OWN)], axis=0)
    picked = dot(rs_ref[...], jnp.concatenate(halves(theta), axis=1), TN).astype(bf16)
    high, low = picked[:, :128], picked[:, 128:]
    rows = jnp.concatenate(
        [jnp.concatenate([high, high], axis=1), jnp.concatenate([low, low], axis=1)], axis=0
    )
    lab = lab_ref[...]

    def weigh(group, carry):
        means = dot(rows, together(e_ref, group, 256), NN)
        means = means[:LABELS] + means[LABELS:]
        par_rows, inverse = rows_of(par_ref, group), rows_of(rinv_ref, group)
        out = []
        for q in range(8):
            mine = lab == par_rows[q : q + 1]
            out.append(jnp.sum(jnp.where(mine, means[:, q * 128 : (q + 1) * 128], 0.0), axis=0, keepdims=True))
        put_rows(tfine, group, [jnp.concatenate(out, axis=0) * inverse])
        return carry

    lax.fori_loop(0, GROUPS, weigh, 0, unroll=UNROLL)
    beside = misc.T
    t = t_ref[...]
    grid[1:5, 8:24, :] = t.reshape(4, 16, 128)
    grid[5, 8:24, :] = beside[64:80]
    grid[0, 8:24, :] = beside[80:96]
    for x in range(4):
        grid[1 + x, 24:25, :] = beside[96 + x : 97 + x]
        grid[1 + x, 7:8, :] = beside[100 + x : 101 + x]
    around = grid[2:6, 8:24, :] + grid[0:4, 8:24, :]
    around = around + grid[1:5, 9:25, :] + grid[1:5, 7:23, :]
    around = around.reshape(ROWS, 128)
    lane = iota((ROWS, 128), 1)
    around = around + jnp.where(lane == 127, 0.0, pltpu.roll(t, 127, 1))
    around = around + jnp.where(lane == 0, 0.0, pltpu.roll(t, 1, 1))
    return t + thermal_diffusion * (around - 6.0 * t) + damping_contribution * (tfine[...] - t)


def middle_kernel(
    got_ref, t_ref, e_ref, rinv_ref, mb_ref, lab_ref, rs_ref, m_ref, par_ref, who_ref,
    t_out, pay, tfine, grid, flux, acc, edge,
):
    misc = got_ref[pl.ds(OWN, 128, stride=LATER), :]
    t = fine_update(got_ref, misc, t_ref, e_ref, rinv_ref, lab_ref, rs_ref, par_ref, tfine, grid)
    t_out[...] = t
    flux[...] = mb_ref[...] * (1.0 + 0.5 * jnp.tanh(t))
    acc[...] = jnp.zeros_like(acc)

    def gather(group, carry):
        flux_rows = rows_of(flux, group)
        arms = []
        for q in range(8):
            mine = who_ref[group * 8 + q]
            arms.append(jnp.concatenate([mine * part for part in halves(flux_rows[q : q + 1])], axis=0))
        acc[...] += dot(jnp.concatenate(arms, axis=1), together(e_ref, group, 128), NT)
        return carry

    lax.fori_loop(0, GROUPS, gather, 0, unroll=UNROLL)
    both = acc[...]
    sums = to_slots(rs_ref[...], both[0:48] + both[48:96])
    for k in range(OWN):
        pay[pl.ds(k, 128, stride=LATER), :] = sums[k * 128 : (k + 1) * 128]
    out = neighbour_sums(misc, m_ref[...]) + edges_by_z(t_out, edge)
    pay[pl.ds(OWN, 128, stride=LATER), :] = out


def final_kernel(
    got_ref, t_ref, e_ref, rinv_ref, lab_ref, rs_ref, par_ref, state_ref, t_out, state_out, tfine, grid
):
    state_out[...] = state_ref[...]
    misc = got_ref[pl.ds(OWN, 128, stride=LATER), :]
    t_out[...] = fine_update(got_ref, misc, t_ref, e_ref, rinv_ref, lab_ref, rs_ref, par_ref, tfine, grid)


def call(kernel, outs, scratch, *operands, scalars=0, results=(), streamed=()):
    vmem, smem = pl.BlockSpec(memory_space=pltpu.VMEM), pl.BlockSpec(memory_space=pltpu.SMEM)
    away = set(results) | set(streamed)
    return pl.pallas_call(
        kernel,
        out_shape=[pltpu.HBM(*o) if i in away else pltpu.VMEM(*o) for i, o in enumerate(outs)],
        in_specs=[smem] * scalars + [vmem] * (len(operands) - scalars),
        out_specs=[pl.BlockSpec(memory_space=pl.ANY) if i in streamed else vmem for i in range(len(outs))],
        scratch_shapes=[pltpu.VMEM(*s) if isinstance(s, tuple) else s for s in scratch],
        compiler_params=pltpu.CompilerParams(vmem_limit_bytes=24 << 20),
    )(*operands)


def exchange(array):
    rows = array.shape[0] // DEV
    sent = array.reshape(DEV, 1, rows * 128)
    return lax.all_to_all(sent, ("gx", "gy"), 0, 0, tiled=True).reshape(array.shape)


def from_hbm(*arrays):
    return [pltpu.with_memory_space_constraint(a, pltpu.HBM) for a in arrays]


def shards(thermal, average, variance, mass, bare, parent, species, position, partners, increments, chem, weight):
    dev = (lax.axis_index("gx") * 8 + lax.axis_index("gy")).astype(jnp.int32).reshape(1)
    fine = [a.reshape(ROWS, 128) for a in (thermal, average, variance, mass, bare, parent)]
    t0, av, var, mass, bare, par = fine
    state = species.reshape(ROWS, ETA)
    bp, ri, sw = position.reshape(1, SLOTS), increments.reshape(1, SLOTS), weight.reshape(1, SPEC)
    cells = ((ROWS, 128), f32)
    square = ((128, 128), f32)
    pay = ((DEV * LATER, 128), f32)

    inputs = from_hbm(state, t0, av, var, mass, bare, par, bp, partners.T, ri, chem, sw)
    *inputs, turned = call(
        load_kernel, [(a.shape, a.dtype) for a in inputs] + [((ETA, ROWS), f32)], [], *inputs, results=(len(inputs),)
    )
    states = lax.all_to_all(turned.reshape(DEV, 1, ROWS), ("gx", "gy"), 0, 0, tiled=True).reshape(DEV, ROWS)
    state, t0, par = inputs[0], inputs[1], inputs[6]
    table, mb, rinv, lab, rs, m, sums, edges, count, cols, sw, who = call(
        prep_kernel,
        [((ROWS, 256, 128), bf16), cells, cells, ((LABELS, 128), jnp.int32), ((SLOTS, LABELS), bf16),
         ((SLOTS, SLOTS), bf16), ((SLOTS, 256), f32), square, cells, ((SPEC, SPEC, ETA), f32), ((SPEC, ETA), f32),
         ((ROWS, LABELS, 128), bf16)],
        [square, square, cells, cells, cells, ((4 * LABELS, 128), f32), ((ROWS, 256, 128), bf16), square, pltpu.SemaphoreType.DMA((GROUPS,))],
        dev, *inputs[1:], scalars=1, streamed=(0,),
    )
    (sent,) = call(first_pack_kernel, [((DEV * FIRST, 128), f32)], [], states, m, sums, edges)
    got = exchange(sent)
    state, own_weight, sent = call(
        first_advance_kernel, [((ROWS, ETA), f32), ((8, 128), f32), pay], [cells],
        got, state, count, cols, sw,
    )
    got = exchange(sent)
    grid = ((6, 32, 128), f32)
    t1, sent = call(
        middle_kernel, [cells, pay],
        [cells, grid, cells, ((2 * LABELS, 128), f32), square],
        got, t0, table, rinv, mb, lab, rs, m, par, who,
    )
    got = exchange(sent)
    state, sent = call(
        later_advance_kernel, [((ROWS, ETA), f32), pay], [cells],
        got, state, own_weight, count, cols, sw,
    )
    got = exchange(sent)
    t2, state = call(
        final_kernel, [cells, cells], [cells, grid], got, t1, table, rinv, lab, rs, par, state, results=(0, 1)
    )
    return state.reshape(species.shape), t2.reshape(thermal.shape)


def solution(mesh):
    fine = P("gx", "gy", None)
    slots = P(("gx", "gy"), None, None)
    return jax.shard_map(
        shards,
        mesh=mesh,
        in_specs=(fine,) * 6 + (slots,) + (P(),) * 5,
        out_specs=(slots, fine),
        check_vma=False,
    )
```

```python
import jax
import jax.numpy as jnp
from jax import lax
from jax.experimental import pallas as pl
from jax.experimental.pallas import tpu as pltpu
from jax.sharding import PartitionSpec as P

DEV = 128
OWN = 4
SLOTS = 512
SPEC = 16
ETA = 128
ROWS = 64
SUBMAX = 16
LABELS = 48
GROUPS = 8
WIDE = 1024
FIRST = 9
LATER = 5
UNROLL = 8
SUBROLL = 4
LOG2E = 1.4426950408889634

coupling = 0.05
mixing_rate = 0.2
react_rate = 0.5
prior_weight = 1.0
prior_flux = 0.5
thermal_diffusion = 0.1
damping_contribution = 0.3

f32 = jnp.float32
bf16 = jnp.bfloat16
NN = ((1,), (0,))
NT = ((1,), (1,))
TN = ((0,), (0,))


def dot(a, b, dims):
    return lax.dot_general(a, b, (dims, ((), ())), preferred_element_type=f32)


def iota(shape, dim):
    return lax.broadcasted_iota(jnp.int32, shape, dim)


def halves(x):
    high = x.astype(bf16)
    return high, (x - high.astype(f32)).astype(bf16)


def hot(mask):
    return jnp.where(mask, 1.0, 0.0).astype(bf16)


def marked(mask):
    return jnp.where(mask, jnp.ones((), bf16), jnp.zeros((), bf16))


def together(ref, group, count):
    return jnp.concatenate([ref[group * 8 + q, 0:count, :] for q in range(8)], axis=1)


def rows_of(ref, group):
    return ref[pl.ds(pl.multiple_of(group * 8, 8), 8), :]


def put_rows(ref, group, rows):
    ref[pl.ds(pl.multiple_of(group * 8, 8), 8), :] = jnp.concatenate(rows, axis=0)


def to_slots(rs, sums):
    both = dot(rs, jnp.concatenate(halves(sums), axis=1), NN)
    return both[:, : sums.shape[1]] + both[:, sums.shape[1] :]


def prep_kernel(
    dev_ref, t_ref, av_ref, var_ref, mass_ref, bare_ref, par_ref, bp_ref, fp_ref, ri_ref, c_ref, sw_ref,
    e_out, mb_ref, rinv_ref, lab_ref, rs_ref, m_ref, sums_ref, edge_ref, count_ref, cols, weight_ref, who_ref, rst_ref,
    le, l1e, a1, b1, chi, over, acc, e_ref, edge, sems,
):
    edge_ref[...] = edges_by_z(t_ref, edge)
    for s in range(SPEC):
        cols[s] = jnp.broadcast_to(c_ref[:, s : s + 1], (SPEC, ETA))
    weight_ref[...] = jnp.broadcast_to(
        jnp.sum(
            jnp.where(iota((SPEC, SPEC), 0) == iota((SPEC, SPEC), 1), sw_ref[...], 0.0), axis=1, keepdims=True
        ),
        (SPEC, ETA),
    )
    own = bp_ref[...] == dev_ref[0] * OWN + (iota((ROWS, SLOTS), 0) >> 4)
    count = jnp.sum(jnp.where(own, ri_ref[...] + 1, 0).astype(f32), axis=1, keepdims=True)
    count_ref[...] = jnp.broadcast_to(count, (ROWS, ETA))

    made = {}

    def label_steps():
        named = jnp.zeros((32, 16), f32)
        for group in range(GROUPS):
            rows = par_ref[group * 8 : (group + 1) * 8, :]
            tall, short = rows >> 4, rows & 15
            tall = jnp.concatenate([hot(tall[q : q + 1] == iota((32, 128), 0)) for q in range(8)], axis=1)
            short = jnp.concatenate([hot(short[q : q + 1] == iota((16, 128), 0)) for q in range(8)], axis=1)
            named = named + dot(tall, short, NT)
        named = hot(named > 0.5)
        yield
        within = dot(named, hot(iota((16, 16), 0) < iota((16, 16), 1)), NN)
        ahead = dot(hot(iota((32, 32), 1) < iota((32, 32), 0)), named, NN).astype(bf16)
        yield
        ahead = dot(ahead, jnp.ones((16, 16), bf16), NN)
        order = jnp.where(named > 0, within + ahead + 1.0, 0.0).astype(bf16)
        yield
        spread = dot(hot(iota((SLOTS, 32), 0) >> 4 == iota((SLOTS, 32), 1)), order, NN)
        spread = jnp.where(iota((SLOTS, 16), 0) & 15 == iota((SLOTS, 16), 1), spread, 0.0).astype(bf16)
        yield
        order = dot(spread, jnp.ones((16, 128), bf16), NN)
        sel = hot(order == (iota((SLOTS, 128), 1) + 1).astype(f32))
        cell = iota((SLOTS, 128), 0) + 1
        yield
        label = dot(
            sel,
            jnp.concatenate([(cell >> 4).astype(f32).astype(bf16), (cell & 15).astype(f32).astype(bf16)], axis=1),
            TN,
        )
        lab = ((label[:, :128] * 16.0 + label[:, 128:]).astype(jnp.int32) - 1)[:LABELS]
        lab_ref[...] = lab
        made['lab'] = lab

        yield
        bp = bp_ref[...]
        device = iota((128, SLOTS), 0).astype(f32).astype(bf16)
        pt = jnp.concatenate(
            [
                marked(jnp.where(bp & 3 == t, bp >> 2, -1).astype(f32).astype(bf16) == device)
                for t in range(OWN)
            ],
            axis=0,
        )
        rs = dot(pt, sel, NN)
        made['rs'] = rs.astype(bf16)[:, :LABELS]
        rst_ref[...] = rs.T[:LABELS].astype(bf16)
        rs_ref[...] = made['rs']
        yield
        other = iota((256, SLOTS), 0).astype(f32).astype(bf16)
        near = fp_ref[...]
        adjacent = []
        for half in range(2):
            part = near - 256 * half
            part = jnp.where((part >= 0) & (part < 256), part, -1).astype(f32)
            total = jnp.zeros((256, SLOTS), bf16)
            for j in range(6):
                total = total + marked(part[j : j + 1].astype(bf16) == other)
            adjacent.append(total)
        half = dot(pt, jnp.concatenate(adjacent, axis=0), NT).astype(bf16)
        m_ref[...] = dot(half, pt, NT).astype(bf16)
        yield

    point = (iota((ETA, 128), 0).astype(f32) + 0.5) / ETA
    le[...] = jnp.log(point) * LOG2E
    l1e[...] = jnp.log(1.0 - point) * LOG2E
    shape_sum = 1.0 / var_ref[...] - 1.0
    a1[...] = av_ref[...] * shape_sum - 1.0
    b1[...] = (1.0 - av_ref[...]) * shape_sum - 1.0
    chi[...] = bare_ref[...] * (1.0 + 0.5 * jnp.tanh(t_ref[...]))

    steps = label_steps()
    for group in range(GROUPS):
        next(steps, None)
        a_rows, b_rows, mass_rows = rows_of(a1, group), rows_of(b1, group), rows_of(mass_ref, group)
        inverse = []
        for q in range(8):
            logits = a_rows[q : q + 1] * le[...] + b_rows[q : q + 1] * l1e[...]
            table = jnp.exp2(logits - jnp.max(logits, axis=0, keepdims=True))
            inverse.append(1.0 / jnp.sum(table, axis=0, keepdims=True))
            high, low = halves(table)
            e_ref[group * 8 + q, 0:128, :] = high
            e_ref[group * 8 + q, 128:256, :] = low
        pltpu.make_async_copy(e_ref.at[pl.ds(group * 8, 8)], e_out.at[pl.ds(group * 8, 8)], sems.at[group]).start()
        inverse = jnp.concatenate(inverse, axis=0)
        put_rows(rinv_ref, group, [inverse])
        put_rows(over, group, [mass_rows * inverse])
        put_rows(mb_ref, group, [mass_rows * inverse * rows_of(bare_ref, group)])
    for _ in steps:
        pass
    lab, rs = made["lab"], made["rs"]
    total = jnp.zeros((4 * LABELS, 128), f32)
    for group in range(GROUPS):
        w_rows, par_rows = rows_of(over, group), rows_of(par_ref, group)
        n_rows = w_rows * rows_of(chi, group)
        arms = []
        for q in range(8):
            mine = hot(lab == par_rows[q : q + 1])
            who_ref[group * 8 + q] = mine
            parts = (*halves(w_rows[q : q + 1]), *halves(n_rows[q : q + 1]))
            arms.append(jnp.concatenate([mine * part for part in parts], axis=0))
        total = total + dot(jnp.concatenate(arms, axis=1), together(e_ref, group, 128), NT)
    acc[...] = total
    both = acc[...]
    w48 = both[0:48] + both[48:96]
    n48 = both[96:144] + both[144:192]
    sums_ref[...] = to_slots(rs, jnp.concatenate([w48, n48], axis=1))
    for group in range(GROUPS):
        pltpu.make_async_copy(e_ref.at[pl.ds(group * 8, 8)], e_out.at[pl.ds(group * 8, 8)], sems.at[group]).wait()


def neighbour_sums(part, m):
    lane = iota((128, 128), 1)
    stacked = jnp.concatenate([jnp.where(lane >> 4 == t, part, 0.0) for t in range(OWN)], axis=0)
    high, low = halves(stacked)
    both = dot(m, jnp.concatenate([high, low], axis=1), NN)
    total = both[:, :128] + both[:, 128:]
    for shift in (64, 32, 16):
        total = total + pltpu.roll(total, shift, 1)
    out = jnp.zeros((128, 128), f32)
    for t in range(OWN):
        out = jnp.where(lane >> 4 == t, total[t * 128 : (t + 1) * 128], out)
    return out


def edges_by_z(t_ref, edge):
    edge[...] = jnp.zeros_like(edge)
    edge[64:80, :] = t_ref[0:16, :]
    edge[80:96, :] = t_ref[48:64, :]
    for x in range(4):
        edge[96 + x : 97 + x, :] = t_ref[16 * x : 16 * x + 1, :]
        edge[100 + x : 101 + x, :] = t_ref[16 * x + 15 : 16 * x + 16, :]
    return edge[...].T


def load_kernel(*refs):
    half = (len(refs) - 1) // 2
    for source, target in zip(refs[:half], refs[half:]):
        target[...] = source[...]
    state = refs[0][...]
    refs[-1][...] = jnp.concatenate([state, state], axis=0).T[:, :ROWS]


def first_pack_kernel(got_ref, m_ref, sums_ref, edge_ref, out_ref):
    misc = neighbour_sums(jnp.concatenate([got_ref[...], jnp.zeros((128, 128 - ROWS), f32)], axis=1), m_ref[...]) + edge_ref[...]
    for t in range(OWN):
        out_ref[pl.ds(t, 128, stride=FIRST), :] = sums_ref[t * 128 : (t + 1) * 128, 0:128]
        out_ref[pl.ds(OWN + t, 128, stride=FIRST), :] = sums_ref[t * 128 : (t + 1) * 128, 128:256]
    out_ref[pl.ds(2 * OWN, 128, stride=FIRST), :] = misc


def passed_on(misc):
    lane, row = iota((128, 128), 1), iota((128, 128), 0)
    gx, gy = row >> 3, row & 7
    out = jnp.where((lane >= 64) & (lane < 80) & (gx < 15), pltpu.roll(misc, 120, 0), 0.0)
    out = jnp.where((lane >= 80) & (lane < 96) & (gx > 0), pltpu.roll(misc, 8, 0), out)
    out = jnp.where((lane >= 96) & (lane < 100) & (gy < 7), pltpu.roll(misc, 127, 0), out)
    return jnp.where((lane >= 100) & (lane < 104) & (gy > 0), pltpu.roll(misc, 1, 0), out)


def advance(state_ref, misc, cchi, count_ref, cols, weight_ref, speed_ref, out_ref, last):
    count = count_ref[...]
    fraction = 1.0 / count
    mixing = fraction * mixing_rate * jnp.concatenate(
        [jnp.broadcast_to(cchi[t], (SPEC, ETA)) for t in range(OWN)], axis=0
    )
    reacting = fraction * react_rate
    near = misc.T[:ROWS]
    state = state_ref[...]
    state = state + coupling * (near - 6.0 * state)
    lane = iota((8, ETA), 1)
    pieces = [slice(p * 8, (p + 1) * 8) for p in range(8)]

    def substep(index, states):
        for p, current in enumerate(states):
            speed_ref[pieces[p]] = jnp.tanh(current)
        out = list(states)
        for t in range(OWN):
            speed = [speed_ref[pl.ds(t * SPEC + s, 8, stride=0), :] for s in range(SPEC)]
            for half in range(2):
                p = 2 * t + half
                current = states[p]
                parts = [speed[s] * cols[s, half * 8 : half * 8 + 8] for s in range(SPEC)]
                while len(parts) > 1:
                    parts = [a + b for a, b in zip(parts[::2], parts[1::2])]
                left = jnp.where(lane == 0, current, pltpu.roll(current, 1, 1))
                right = jnp.where(lane == ETA - 1, current, pltpu.roll(current, ETA - 1, 1))
                update = mixing[pieces[p]] * (right - 2.0 * current + left) + reacting[pieces[p]] * parts[0]
                out[p] = jnp.where(index.astype(f32) < count[pieces[p]], current + update, current)
        return tuple(out)

    state = jnp.concatenate(
        lax.fori_loop(0, SUBMAX, substep, tuple(state[p] for p in pieces), unroll=SUBROLL), axis=0
    )
    state_ref_out, pay = out_ref
    state_ref_out[...] = state
    weight = weight_ref[...]
    for t in range(OWN):
        theta = jnp.sum(weight * state[t * SPEC : (t + 1) * SPEC], axis=0, keepdims=True)
        pay[pl.ds(t, 128, stride=LATER), :] = jnp.broadcast_to(theta, (128, ETA))
    out = passed_on(misc)
    if not last:
        out = out + jnp.concatenate([state, jnp.zeros((128 - ROWS, ETA), f32)], axis=0).T
    pay[pl.ds(OWN, 128, stride=LATER), :] = out


def total_of(got_ref, row, stride):
    return jnp.sum(got_ref[pl.ds(row, 128, stride=stride), :], axis=0, keepdims=True)


def first_advance_kernel(
    got_ref, state_ref, count_ref, cols, weight_ref, state_out, weight_out, pay, speed_ref
):
    cchi = []
    for t in range(OWN):
        w = total_of(got_ref, t, FIRST)
        n = total_of(got_ref, OWN + t, FIRST)
        weight_out[t : t + 1, :] = w
        cchi.append((n + prior_flux) / (w + prior_weight))
    misc = got_ref[pl.ds(2 * OWN, 128, stride=FIRST), :]
    advance(state_ref, misc, cchi, count_ref, cols, weight_ref, speed_ref, (state_out, pay), False)


def later_advance_kernel(
    got_ref, state_ref, mass_ref, count_ref, cols, weight_ref, state_out, pay, speed_ref
):
    cchi = []
    for t in range(OWN):
        n = total_of(got_ref, t, LATER)
        cchi.append((n + prior_flux) / (mass_ref[t : t + 1, :] + prior_weight))
    misc = got_ref[pl.ds(OWN, 128, stride=LATER), :]
    advance(state_ref, misc, cchi, count_ref, cols, weight_ref, speed_ref, (state_out, pay), True)


def fine_update(got_ref, misc, t_ref, e_ref, rinv_ref, lab_ref, rst_ref, par_ref, tfine, grid):
    theta = jnp.concatenate([got_ref[pl.ds(t, 128, stride=LATER), :] for t in range(OWN)], axis=0)
    picked = dot(rst_ref[...], jnp.concatenate(halves(theta), axis=1), NN).astype(bf16)
    high, low = picked[:, :128], picked[:, 128:]
    rows = jnp.concatenate(
        [jnp.concatenate([high, high], axis=1), jnp.concatenate([low, low], axis=1)], axis=0
    )
    lab = lab_ref[...]

    def weigh(group, carry):
        means = dot(rows, together(e_ref, group, 256), NN)
        means = means[:LABELS] + means[LABELS:]
        par_rows, inverse = rows_of(par_ref, group), rows_of(rinv_ref, group)
        out = []
        for q in range(8):
            mine = lab == par_rows[q : q + 1]
            out.append(jnp.sum(jnp.where(mine, means[:, q * 128 : (q + 1) * 128], 0.0), axis=0, keepdims=True))
        put_rows(tfine, group, [jnp.concatenate(out, axis=0) * inverse])
        return carry

    lax.fori_loop(0, GROUPS, weigh, 0, unroll=UNROLL)
    beside = misc.T
    t = t_ref[...]
    grid[1:5, 8:24, :] = t.reshape(4, 16, 128)
    grid[5, 8:24, :] = beside[64:80]
    grid[0, 8:24, :] = beside[80:96]
    for x in range(4):
        grid[1 + x, 24:25, :] = beside[96 + x : 97 + x]
        grid[1 + x, 7:8, :] = beside[100 + x : 101 + x]
    around = grid[2:6, 8:24, :] + grid[0:4, 8:24, :]
    around = around + grid[1:5, 9:25, :] + grid[1:5, 7:23, :]
    around = around.reshape(ROWS, 128)
    lane = iota((ROWS, 128), 1)
    around = around + jnp.where(lane == 127, 0.0, pltpu.roll(t, 127, 1))
    around = around + jnp.where(lane == 0, 0.0, pltpu.roll(t, 1, 1))
    return t + thermal_diffusion * (around - 6.0 * t) + damping_contribution * (tfine[...] - t)


def middle_kernel(
    got_ref, t_ref, e_ref, rinv_ref, mb_ref, lab_ref, rs_ref, rst_ref, m_ref, par_ref, who_ref,
    t_out, pay, tfine, grid, flux, acc, edge,
):
    misc = got_ref[pl.ds(OWN, 128, stride=LATER), :]
    near = neighbour_sums(misc, m_ref[...])
    t = fine_update(got_ref, misc, t_ref, e_ref, rinv_ref, lab_ref, rst_ref, par_ref, tfine, grid)
    t_out[...] = t
    pay[pl.ds(OWN, 128, stride=LATER), :] = near + edges_by_z(t_out, edge)
    flux[...] = mb_ref[...] * (1.0 + 0.5 * jnp.tanh(t))
    acc[...] = jnp.zeros_like(acc)

    def gather(group, carry):
        flux_rows = rows_of(flux, group)
        arms = []
        for q in range(8):
            mine = who_ref[group * 8 + q]
            arms.append(jnp.concatenate([mine * part for part in halves(flux_rows[q : q + 1])], axis=0))
        acc[...] += dot(jnp.concatenate(arms, axis=1), together(e_ref, group, 128), NT)
        return carry

    lax.fori_loop(0, GROUPS, gather, 0, unroll=UNROLL)
    both = acc[...]
    sums = to_slots(rs_ref[...], both[0:48] + both[48:96])
    for k in range(OWN):
        pay[pl.ds(k, 128, stride=LATER), :] = sums[k * 128 : (k + 1) * 128]


def final_kernel(
    got_ref, t_ref, e_ref, rinv_ref, lab_ref, rst_ref, par_ref, state_ref, t_out, state_out, tfine, grid
):
    state_out[...] = state_ref[...]
    misc = got_ref[pl.ds(OWN, 128, stride=LATER), :]
    t_out[...] = fine_update(got_ref, misc, t_ref, e_ref, rinv_ref, lab_ref, rst_ref, par_ref, tfine, grid)


def call(kernel, outs, scratch, *operands, scalars=0, results=(), streamed=()):
    vmem, smem = pl.BlockSpec(memory_space=pltpu.VMEM), pl.BlockSpec(memory_space=pltpu.SMEM)
    away = set(results) | set(streamed)
    return pl.pallas_call(
        kernel,
        out_shape=[pltpu.HBM(*o) if i in away else pltpu.VMEM(*o) for i, o in enumerate(outs)],
        in_specs=[smem] * scalars + [vmem] * (len(operands) - scalars),
        out_specs=[pl.BlockSpec(memory_space=pl.ANY) if i in streamed else vmem for i in range(len(outs))],
        scratch_shapes=[pltpu.VMEM(*s) if isinstance(s, tuple) else s for s in scratch],
        compiler_params=pltpu.CompilerParams(vmem_limit_bytes=24 << 20),
    )(*operands)


def exchange(array):
    rows = array.shape[0] // DEV
    sent = array.reshape(DEV, 1, rows * 128)
    return lax.all_to_all(sent, ("gx", "gy"), 0, 0, tiled=True).reshape(array.shape)


def from_hbm(*arrays):
    return [pltpu.with_memory_space_constraint(a, pltpu.HBM) for a in arrays]


def shards(thermal, average, variance, mass, bare, parent, species, position, partners, increments, chem, weight):
    dev = (lax.axis_index("gx") * 8 + lax.axis_index("gy")).astype(jnp.int32).reshape(1)
    fine = [a.reshape(ROWS, 128) for a in (thermal, average, variance, mass, bare, parent)]
    t0, av, var, mass, bare, par = fine
    state = species.reshape(ROWS, ETA)
    bp, ri, sw = position.reshape(1, SLOTS), increments.reshape(1, SLOTS), weight.reshape(1, SPEC)
    cells = ((ROWS, 128), f32)
    square = ((128, 128), f32)
    pay = ((DEV * LATER, 128), f32)

    inputs = from_hbm(state, t0, av, var, mass, bare, par, bp, partners.T, ri, chem, sw)
    *inputs, turned = call(
        load_kernel, [(a.shape, a.dtype) for a in inputs] + [((ETA, ROWS), f32)], [], *inputs, results=(len(inputs),)
    )
    states = lax.all_to_all(turned.reshape(DEV, 1, ROWS), ("gx", "gy"), 0, 0, tiled=True).reshape(DEV, ROWS)
    state, t0, par = inputs[0], inputs[1], inputs[6]
    table, mb, rinv, lab, rs, m, sums, edges, count, cols, sw, who, rst = call(
        prep_kernel,
        [((ROWS, 256, 128), bf16), cells, cells, ((LABELS, 128), jnp.int32), ((SLOTS, LABELS), bf16),
         ((SLOTS, SLOTS), bf16), ((SLOTS, 256), f32), square, cells, ((SPEC, SPEC, ETA), f32), ((SPEC, ETA), f32),
         ((ROWS, LABELS, 128), bf16), ((LABELS, SLOTS), bf16)],
        [square, square, cells, cells, cells, cells, ((4 * LABELS, 128), f32), ((ROWS, 256, 128), bf16), square, pltpu.SemaphoreType.DMA((GROUPS,))],
        dev, *inputs[1:], scalars=1, streamed=(0,),
    )
    (sent,) = call(first_pack_kernel, [((DEV * FIRST, 128), f32)], [], states, m, sums, edges)
    got = exchange(sent)
    state, own_weight, sent = call(
        first_advance_kernel, [((ROWS, ETA), f32), ((8, 128), f32), pay], [cells],
        got, state, count, cols, sw,
    )
    got = exchange(sent)
    grid = ((6, 32, 128), f32)
    t1, sent = call(
        middle_kernel, [cells, pay],
        [cells, grid, cells, ((2 * LABELS, 128), f32), square],
        got, t0, table, rinv, mb, lab, rs, rst, m, par, who,
    )
    got = exchange(sent)
    state, sent = call(
        later_advance_kernel, [((ROWS, ETA), f32), pay], [cells],
        got, state, own_weight, count, cols, sw,
    )
    got = exchange(sent)
    t2, state = call(
        final_kernel, [cells, cells], [cells, grid], got, t1, table, rinv, lab, rst, par, state, results=(0, 1)
    )
    return state.reshape(species.shape), t2.reshape(thermal.shape)


def solution(mesh):
    fine = P("gx", "gy", None)
    slots = P(("gx", "gy"), None, None)
    return jax.shard_map(
        shards,
        mesh=mesh,
        in_specs=(fine,) * 6 + (slots,) + (P(),) * 5,
        out_specs=(slots, fine),
        check_vma=False,
    )
```

```python
import jax
import jax.numpy as jnp
from jax import lax
from jax.experimental import pallas as pl
from jax.experimental.pallas import tpu as pltpu
from jax.sharding import PartitionSpec as P

DEV = 128
OWN = 4
SLOTS = 512
SPEC = 16
ETA = 128
ROWS = 64
SUBMAX = 16
LABELS = 48
GROUPS = 8
WIDE = 1024
FIRST = 9
LATER = 5
UNROLL = 8
SUBROLL = 16
LOG2E = 1.4426950408889634

coupling = 0.05
mixing_rate = 0.2
react_rate = 0.5
prior_weight = 1.0
prior_flux = 0.5
thermal_diffusion = 0.1
damping_contribution = 0.3

f32 = jnp.float32
bf16 = jnp.bfloat16
NN = ((1,), (0,))
NT = ((1,), (1,))
TN = ((0,), (0,))


def dot(a, b, dims):
    return lax.dot_general(a, b, (dims, ((), ())), preferred_element_type=f32)


def iota(shape, dim):
    return lax.broadcasted_iota(jnp.int32, shape, dim)


def halves(x):
    high = x.astype(bf16)
    return high, (x - high.astype(f32)).astype(bf16)


def hot(mask):
    return jnp.where(mask, 1.0, 0.0).astype(bf16)


def marked(mask):
    return jnp.where(mask, jnp.ones((), bf16), jnp.zeros((), bf16))


def together(ref, group, count):
    return jnp.concatenate([ref[group * 8 + q, 0:count, :] for q in range(8)], axis=1)


def rows_of(ref, group):
    return ref[pl.ds(pl.multiple_of(group * 8, 8), 8), :]


def put_rows(ref, group, rows):
    ref[pl.ds(pl.multiple_of(group * 8, 8), 8), :] = jnp.concatenate(rows, axis=0)


def to_slots(rs, sums):
    both = dot(rs, jnp.concatenate(halves(sums), axis=1), NN)
    return both[:, : sums.shape[1]] + both[:, sums.shape[1] :]


def prep_kernel(
    dev_ref, t_ref, av_ref, var_ref, mass_ref, bare_ref, par_ref, bp_ref, fp_ref, ri_ref, c_ref, sw_ref,
    e_out, mb_ref, rinv_ref, lab_ref, rs_ref, m_ref, sums_ref, edge_ref, count_ref, cols, weight_ref, who_ref, rst_ref,
    le, l1e, a1, b1, chi, over, acc, e_ref, edge, sems,
):
    edge_ref[...] = edges_by_z(t_ref, edge)
    for s in range(SPEC):
        cols[s] = jnp.broadcast_to(c_ref[:, s : s + 1], (SPEC, ETA))
    weight_ref[...] = jnp.broadcast_to(
        jnp.sum(
            jnp.where(iota((SPEC, SPEC), 0) == iota((SPEC, SPEC), 1), sw_ref[...], 0.0), axis=1, keepdims=True
        ),
        (SPEC, ETA),
    )
    own = bp_ref[...] == dev_ref[0] * OWN + (iota((ROWS, SLOTS), 0) >> 4)
    count = jnp.sum(jnp.where(own, ri_ref[...] + 1, 0).astype(f32), axis=1, keepdims=True)
    count_ref[...] = jnp.broadcast_to(count, (ROWS, ETA))

    made = {}

    def label_steps():
        named = jnp.zeros((32, 16), f32)
        for group in range(GROUPS):
            rows = par_ref[group * 8 : (group + 1) * 8, :]
            tall, short = rows >> 4, rows & 15
            tall = jnp.concatenate([hot(tall[q : q + 1] == iota((32, 128), 0)) for q in range(8)], axis=1)
            short = jnp.concatenate([hot(short[q : q + 1] == iota((16, 128), 0)) for q in range(8)], axis=1)
            named = named + dot(tall, short, NT)
        named = hot(named > 0.5)
        yield
        within = dot(named, hot(iota((16, 16), 0) < iota((16, 16), 1)), NN)
        ahead = dot(hot(iota((32, 32), 1) < iota((32, 32), 0)), named, NN).astype(bf16)
        yield
        ahead = dot(ahead, jnp.ones((16, 16), bf16), NN)
        order = jnp.where(named > 0, within + ahead + 1.0, 0.0).astype(bf16)
        yield
        spread = dot(hot(iota((SLOTS, 32), 0) >> 4 == iota((SLOTS, 32), 1)), order, NN)
        spread = jnp.where(iota((SLOTS, 16), 0) & 15 == iota((SLOTS, 16), 1), spread, 0.0).astype(bf16)
        yield
        order = dot(spread, jnp.ones((16, 128), bf16), NN)
        sel = hot(order == (iota((SLOTS, 128), 1) + 1).astype(f32))
        cell = iota((SLOTS, 128), 0) + 1
        yield
        label = dot(
            sel,
            jnp.concatenate([(cell >> 4).astype(f32).astype(bf16), (cell & 15).astype(f32).astype(bf16)], axis=1),
            TN,
        )
        lab = ((label[:, :128] * 16.0 + label[:, 128:]).astype(jnp.int32) - 1)[:LABELS]
        lab_ref[...] = lab
        made['lab'] = lab

        yield
        bp = bp_ref[...]
        device = iota((128, SLOTS), 0).astype(f32).astype(bf16)
        pt = jnp.concatenate(
            [
                marked(jnp.where(bp & 3 == t, bp >> 2, -1).astype(f32).astype(bf16) == device)
                for t in range(OWN)
            ],
            axis=0,
        )
        rs = dot(pt, sel, NN)
        made['rs'] = rs.astype(bf16)[:, :LABELS]
        rst_ref[...] = rs.T[:LABELS].astype(bf16)
        rs_ref[...] = made['rs']
        yield
        other = iota((256, SLOTS), 0).astype(f32).astype(bf16)
        near = fp_ref[...]
        adjacent = []
        for half in range(2):
            part = near - 256 * half
            part = jnp.where((part >= 0) & (part < 256), part, -1).astype(f32)
            total = jnp.zeros((256, SLOTS), bf16)
            for j in range(6):
                total = total + marked(part[j : j + 1].astype(bf16) == other)
            adjacent.append(total)
        half = dot(pt, jnp.concatenate(adjacent, axis=0), NT).astype(bf16)
        m_ref[...] = dot(half, pt, NT).astype(bf16)
        yield

    point = (iota((ETA, 128), 0).astype(f32) + 0.5) / ETA
    le[...] = jnp.log(point) * LOG2E
    l1e[...] = jnp.log(1.0 - point) * LOG2E
    shape_sum = 1.0 / var_ref[...] - 1.0
    a1[...] = av_ref[...] * shape_sum - 1.0
    b1[...] = (1.0 - av_ref[...]) * shape_sum - 1.0
    chi[...] = bare_ref[...] * (1.0 + 0.5 * jnp.tanh(t_ref[...]))

    steps = label_steps()
    for group in range(GROUPS):
        next(steps, None)
        a_rows, b_rows, mass_rows = rows_of(a1, group), rows_of(b1, group), rows_of(mass_ref, group)
        inverse = []
        for q in range(8):
            logits = a_rows[q : q + 1] * le[...] + b_rows[q : q + 1] * l1e[...]
            table = jnp.exp2(logits - jnp.max(logits, axis=0, keepdims=True))
            inverse.append(1.0 / jnp.sum(table, axis=0, keepdims=True))
            high, low = halves(table)
            e_ref[group * 8 + q, 0:128, :] = high
            e_ref[group * 8 + q, 128:256, :] = low
        pltpu.make_async_copy(e_ref.at[pl.ds(group * 8, 8)], e_out.at[pl.ds(group * 8, 8)], sems.at[group]).start()
        inverse = jnp.concatenate(inverse, axis=0)
        put_rows(rinv_ref, group, [inverse])
        put_rows(over, group, [mass_rows * inverse])
        put_rows(mb_ref, group, [mass_rows * inverse * rows_of(bare_ref, group)])
    for _ in steps:
        pass
    lab, rs = made["lab"], made["rs"]
    total = jnp.zeros((4 * LABELS, 128), f32)
    for group in range(GROUPS):
        w_rows, par_rows = rows_of(over, group), rows_of(par_ref, group)
        n_rows = w_rows * rows_of(chi, group)
        arms = []
        for q in range(8):
            mine = hot(lab == par_rows[q : q + 1])
            who_ref[group * 8 + q] = mine
            parts = (*halves(w_rows[q : q + 1]), *halves(n_rows[q : q + 1]))
            arms.append(jnp.concatenate([mine * part for part in parts], axis=0))
        total = total + dot(jnp.concatenate(arms, axis=1), together(e_ref, group, 128), NT)
    acc[...] = total
    both = acc[...]
    w48 = both[0:48] + both[48:96]
    n48 = both[96:144] + both[144:192]
    sums_ref[...] = to_slots(rs, jnp.concatenate([w48, n48], axis=1))
    for group in range(GROUPS):
        pltpu.make_async_copy(e_ref.at[pl.ds(group * 8, 8)], e_out.at[pl.ds(group * 8, 8)], sems.at[group]).wait()


def neighbour_sums(part, m):
    lane = iota((128, 128), 1)
    stacked = jnp.concatenate([jnp.where(lane >> 4 == t, part, 0.0) for t in range(OWN)], axis=0)
    high, low = halves(stacked)
    both = dot(m, jnp.concatenate([high, low], axis=1), NN)
    total = both[:, :128] + both[:, 128:]
    for shift in (64, 32, 16):
        total = total + pltpu.roll(total, shift, 1)
    out = jnp.zeros((128, 128), f32)
    for t in range(OWN):
        out = jnp.where(lane >> 4 == t, total[t * 128 : (t + 1) * 128], out)
    return out


def edges_by_z(t_ref, edge):
    edge[...] = jnp.zeros_like(edge)
    edge[64:80, :] = t_ref[0:16, :]
    edge[80:96, :] = t_ref[48:64, :]
    for x in range(4):
        edge[96 + x : 97 + x, :] = t_ref[16 * x : 16 * x + 1, :]
        edge[100 + x : 101 + x, :] = t_ref[16 * x + 15 : 16 * x + 16, :]
    return edge[...].T


def load_kernel(*refs):
    half = (len(refs) - 1) // 2
    for source, target in zip(refs[:half], refs[half:]):
        target[...] = source[...]
    state = refs[0][...]
    refs[-1][...] = jnp.concatenate([state, state], axis=0).T[:, :ROWS]


def first_pack_kernel(got_ref, m_ref, sums_ref, edge_ref, out_ref):
    misc = neighbour_sums(jnp.concatenate([got_ref[...], jnp.zeros((128, 128 - ROWS), f32)], axis=1), m_ref[...]) + edge_ref[...]
    for t in range(OWN):
        out_ref[pl.ds(t, 128, stride=FIRST), :] = sums_ref[t * 128 : (t + 1) * 128, 0:128]
        out_ref[pl.ds(OWN + t, 128, stride=FIRST), :] = sums_ref[t * 128 : (t + 1) * 128, 128:256]
    out_ref[pl.ds(2 * OWN, 128, stride=FIRST), :] = misc


def passed_on(misc):
    lane, row = iota((128, 128), 1), iota((128, 128), 0)
    gx, gy = row >> 3, row & 7
    out = jnp.where((lane >= 64) & (lane < 80) & (gx < 15), pltpu.roll(misc, 120, 0), 0.0)
    out = jnp.where((lane >= 80) & (lane < 96) & (gx > 0), pltpu.roll(misc, 8, 0), out)
    out = jnp.where((lane >= 96) & (lane < 100) & (gy < 7), pltpu.roll(misc, 127, 0), out)
    return jnp.where((lane >= 100) & (lane < 104) & (gy > 0), pltpu.roll(misc, 1, 0), out)


def advance(state_ref, misc, cchi, count_ref, cols, weight_ref, speed_ref, out_ref, last):
    count = count_ref[...]
    fraction = 1.0 / count
    mixing = fraction * mixing_rate * jnp.concatenate(
        [jnp.broadcast_to(cchi[t], (SPEC, ETA)) for t in range(OWN)], axis=0
    )
    reacting = fraction * react_rate
    near = misc.T[:ROWS]
    state = state_ref[...]
    state = state + coupling * (near - 6.0 * state)
    lane = iota((8, ETA), 1)
    pieces = [slice(p * 8, (p + 1) * 8) for p in range(8)]

    def substep(index, states):
        for p, current in enumerate(states):
            speed_ref[pieces[p]] = jnp.tanh(current)
        out = list(states)
        for t in range(OWN):
            speed = [speed_ref[pl.ds(t * SPEC + s, 8, stride=0), :] for s in range(SPEC)]
            for half in range(2):
                p = 2 * t + half
                current = states[p]
                parts = [speed[s] * cols[s, half * 8 : half * 8 + 8] for s in range(SPEC)]
                while len(parts) > 1:
                    parts = [a + b for a, b in zip(parts[::2], parts[1::2])]
                left = jnp.where(lane == 0, current, pltpu.roll(current, 1, 1))
                right = jnp.where(lane == ETA - 1, current, pltpu.roll(current, ETA - 1, 1))
                update = mixing[pieces[p]] * (right - 2.0 * current + left) + reacting[pieces[p]] * parts[0]
                out[p] = jnp.where(index.astype(f32) < count[pieces[p]], current + update, current)
        return tuple(out)

    state = jnp.concatenate(
        lax.fori_loop(0, SUBMAX, substep, tuple(state[p] for p in pieces), unroll=SUBROLL), axis=0
    )
    state_ref_out, pay = out_ref
    state_ref_out[...] = state
    weight = weight_ref[...]
    for t in range(OWN):
        theta = jnp.sum(weight * state[t * SPEC : (t + 1) * SPEC], axis=0, keepdims=True)
        pay[pl.ds(t, 128, stride=LATER), :] = jnp.broadcast_to(theta, (128, ETA))
    out = passed_on(misc)
    if not last:
        out = out + jnp.concatenate([state, jnp.zeros((128 - ROWS, ETA), f32)], axis=0).T
    pay[pl.ds(OWN, 128, stride=LATER), :] = out


def total_of(got_ref, row, stride):
    return jnp.sum(got_ref[pl.ds(row, 128, stride=stride), :], axis=0, keepdims=True)


def first_advance_kernel(
    got_ref, state_ref, count_ref, cols, weight_ref, state_out, weight_out, pay, speed_ref
):
    cchi = []
    for t in range(OWN):
        w = total_of(got_ref, t, FIRST)
        n = total_of(got_ref, OWN + t, FIRST)
        weight_out[t : t + 1, :] = w
        cchi.append((n + prior_flux) / (w + prior_weight))
    misc = got_ref[pl.ds(2 * OWN, 128, stride=FIRST), :]
    advance(state_ref, misc, cchi, count_ref, cols, weight_ref, speed_ref, (state_out, pay), False)


def later_advance_kernel(
    got_ref, state_ref, mass_ref, count_ref, cols, weight_ref, state_out, pay, speed_ref
):
    cchi = []
    for t in range(OWN):
        n = total_of(got_ref, t, LATER)
        cchi.append((n + prior_flux) / (mass_ref[t : t + 1, :] + prior_weight))
    misc = got_ref[pl.ds(OWN, 128, stride=LATER), :]
    advance(state_ref, misc, cchi, count_ref, cols, weight_ref, speed_ref, (state_out, pay), True)


def fine_update(got_ref, misc, t_ref, e_ref, rinv_ref, lab_ref, rst_ref, par_ref, tfine, grid):
    theta = jnp.concatenate([got_ref[pl.ds(t, 128, stride=LATER), :] for t in range(OWN)], axis=0)
    picked = dot(rst_ref[...], jnp.concatenate(halves(theta), axis=1), NN).astype(bf16)
    high, low = picked[:, :128], picked[:, 128:]
    rows = jnp.concatenate(
        [jnp.concatenate([high, high], axis=1), jnp.concatenate([low, low], axis=1)], axis=0
    )
    lab = lab_ref[...]

    def weigh(group, carry):
        means = dot(rows, together(e_ref, group, 256), NN)
        means = means[:LABELS] + means[LABELS:]
        par_rows, inverse = rows_of(par_ref, group), rows_of(rinv_ref, group)
        out = []
        for q in range(8):
            mine = lab == par_rows[q : q + 1]
            out.append(jnp.sum(jnp.where(mine, means[:, q * 128 : (q + 1) * 128], 0.0), axis=0, keepdims=True))
        put_rows(tfine, group, [jnp.concatenate(out, axis=0) * inverse])
        return carry

    lax.fori_loop(0, GROUPS, weigh, 0, unroll=UNROLL)
    beside = misc.T
    t = t_ref[...]
    grid[1:5, 8:24, :] = t.reshape(4, 16, 128)
    grid[5, 8:24, :] = beside[64:80]
    grid[0, 8:24, :] = beside[80:96]
    for x in range(4):
        grid[1 + x, 24:25, :] = beside[96 + x : 97 + x]
        grid[1 + x, 7:8, :] = beside[100 + x : 101 + x]
    around = grid[2:6, 8:24, :] + grid[0:4, 8:24, :]
    around = around + grid[1:5, 9:25, :] + grid[1:5, 7:23, :]
    around = around.reshape(ROWS, 128)
    lane = iota((ROWS, 128), 1)
    around = around + jnp.where(lane == 127, 0.0, pltpu.roll(t, 127, 1))
    around = around + jnp.where(lane == 0, 0.0, pltpu.roll(t, 1, 1))
    return t + thermal_diffusion * (around - 6.0 * t) + damping_contribution * (tfine[...] - t)


def middle_kernel(
    got_ref, t_ref, e_ref, rinv_ref, mb_ref, lab_ref, rs_ref, rst_ref, m_ref, par_ref, who_ref,
    t_out, pay, tfine, grid, flux, acc, edge,
):
    misc = got_ref[pl.ds(OWN, 128, stride=LATER), :]
    near = neighbour_sums(misc, m_ref[...])
    t = fine_update(got_ref, misc, t_ref, e_ref, rinv_ref, lab_ref, rst_ref, par_ref, tfine, grid)
    t_out[...] = t
    pay[pl.ds(OWN, 128, stride=LATER), :] = near + edges_by_z(t_out, edge)
    flux[...] = mb_ref[...] * (1.0 + 0.5 * jnp.tanh(t))
    acc[...] = jnp.zeros_like(acc)

    def gather(group, carry):
        flux_rows = rows_of(flux, group)
        arms = []
        for q in range(8):
            mine = who_ref[group * 8 + q]
            arms.append(jnp.concatenate([mine * part for part in halves(flux_rows[q : q + 1])], axis=0))
        acc[...] += dot(jnp.concatenate(arms, axis=1), together(e_ref, group, 128), NT)
        return carry

    lax.fori_loop(0, GROUPS, gather, 0, unroll=UNROLL)
    both = acc[...]
    sums = to_slots(rs_ref[...], both[0:48] + both[48:96])
    for k in range(OWN):
        pay[pl.ds(k, 128, stride=LATER), :] = sums[k * 128 : (k + 1) * 128]


def final_kernel(
    got_ref, t_ref, e_ref, rinv_ref, lab_ref, rst_ref, par_ref, state_ref, t_out, state_out, tfine, grid
):
    state_out[...] = state_ref[...]
    misc = got_ref[pl.ds(OWN, 128, stride=LATER), :]
    t_out[...] = fine_update(got_ref, misc, t_ref, e_ref, rinv_ref, lab_ref, rst_ref, par_ref, tfine, grid)


def call(kernel, outs, scratch, *operands, scalars=0, results=(), streamed=()):
    vmem, smem = pl.BlockSpec(memory_space=pltpu.VMEM), pl.BlockSpec(memory_space=pltpu.SMEM)
    away = set(results) | set(streamed)
    return pl.pallas_call(
        kernel,
        out_shape=[pltpu.HBM(*o) if i in away else pltpu.VMEM(*o) for i, o in enumerate(outs)],
        in_specs=[smem] * scalars + [vmem] * (len(operands) - scalars),
        out_specs=[pl.BlockSpec(memory_space=pl.ANY) if i in streamed else vmem for i in range(len(outs))],
        scratch_shapes=[pltpu.VMEM(*s) if isinstance(s, tuple) else s for s in scratch],
        compiler_params=pltpu.CompilerParams(vmem_limit_bytes=24 << 20),
    )(*operands)


def exchange(array):
    rows = array.shape[0] // DEV
    sent = array.reshape(DEV, 1, rows * 128)
    return lax.all_to_all(sent, ("gx", "gy"), 0, 0, tiled=True).reshape(array.shape)


def from_hbm(*arrays):
    return [pltpu.with_memory_space_constraint(a, pltpu.HBM) for a in arrays]


def shards(thermal, average, variance, mass, bare, parent, species, position, partners, increments, chem, weight):
    dev = (lax.axis_index("gx") * 8 + lax.axis_index("gy")).astype(jnp.int32).reshape(1)
    fine = [a.reshape(ROWS, 128) for a in (thermal, average, variance, mass, bare, parent)]
    t0, av, var, mass, bare, par = fine
    state = species.reshape(ROWS, ETA)
    bp, ri, sw = position.reshape(1, SLOTS), increments.reshape(1, SLOTS), weight.reshape(1, SPEC)
    cells = ((ROWS, 128), f32)
    square = ((128, 128), f32)
    pay = ((DEV * LATER, 128), f32)

    inputs = from_hbm(state, t0, av, var, mass, bare, par, bp, partners.T, ri, chem, sw)
    *inputs, turned = call(
        load_kernel, [(a.shape, a.dtype) for a in inputs] + [((ETA, ROWS), f32)], [], *inputs, results=(len(inputs),)
    )
    states = lax.all_to_all(turned.reshape(DEV, 1, ROWS), ("gx", "gy"), 0, 0, tiled=True).reshape(DEV, ROWS)
    state, t0, par = inputs[0], inputs[1], inputs[6]
    table, mb, rinv, lab, rs, m, sums, edges, count, cols, sw, who, rst = call(
        prep_kernel,
        [((ROWS, 256, 128), bf16), cells, cells, ((LABELS, 128), jnp.int32), ((SLOTS, LABELS), bf16),
         ((SLOTS, SLOTS), bf16), ((SLOTS, 256), f32), square, cells, ((SPEC, SPEC, ETA), f32), ((SPEC, ETA), f32),
         ((ROWS, LABELS, 128), bf16), ((LABELS, SLOTS), bf16)],
        [square, square, cells, cells, cells, cells, ((4 * LABELS, 128), f32), ((ROWS, 256, 128), bf16), square, pltpu.SemaphoreType.DMA((GROUPS,))],
        dev, *inputs[1:], scalars=1, streamed=(0,),
    )
    (sent,) = call(first_pack_kernel, [((DEV * FIRST, 128), f32)], [], states, m, sums, edges)
    got = exchange(sent)
    state, own_weight, sent = call(
        first_advance_kernel, [((ROWS, ETA), f32), ((8, 128), f32), pay], [cells],
        got, state, count, cols, sw,
    )
    got = exchange(sent)
    grid = ((6, 32, 128), f32)
    t1, sent = call(
        middle_kernel, [cells, pay],
        [cells, grid, cells, ((2 * LABELS, 128), f32), square],
        got, t0, table, rinv, mb, lab, rs, rst, m, par, who,
    )
    got = exchange(sent)
    state, sent = call(
        later_advance_kernel, [((ROWS, ETA), f32), pay], [cells],
        got, state, own_weight, count, cols, sw,
    )
    got = exchange(sent)
    t2, state = call(
        final_kernel, [cells, cells], [cells, grid], got, t1, table, rinv, lab, rst, par, state, results=(0, 1)
    )
    return state.reshape(species.shape), t2.reshape(thermal.shape)


def solution(mesh):
    fine = P("gx", "gy", None)
    slots = P(("gx", "gy"), None, None)
    return jax.shard_map(
        shards,
        mesh=mesh,
        in_specs=(fine,) * 6 + (slots,) + (P(),) * 5,
        out_specs=(slots, fine),
        check_vma=False,
    )
```
